32 devices in a mesh: dp: 8 (over y, x, core), mp: 4 (over z).
Axes of the slice: x: 2, y: 2, z: 4, core: 2. Of those that a mesh axis runs over, the one named last changes fastest.
Arguments:
- patches: bfloat16 [1024, 588], P('dp'), may hold values from -6 to 6
- embed_weight: bfloat16 [6144, 588], P(('mp', 'dp')), may hold values from -0.25 to 0.25
- project_weight: bfloat16 [6144, 3, 3072], P('dp', None, 'mp'), may hold values from -0.078125 to 0.078125
- patch_counts: int32 [64], P('dp'), may hold values from 0 to 64, as said below
- segment_ids: int32 [1024], P('dp'), may hold values from -1 to 63, as said below
- targets: bfloat16 [1024, 3072], P('dp', 'mp'), may hold values from -4 to 4
Outputs:
- project_grad: float32 [6144, 3, 3072], P('dp', None, 'mp')
- loss_value: float32 [], replicated
The draws below stay inside these ranges and needn't reach their ends.
Inputs may be any that keep to these rules, and one draw needn't show every extreme that they name: `patch_counts`: entry 8 * i + j is the number of patches of image slot j of device i along dp, a multiple of 16, 0 for an empty slot; the counts of one device add up to at most 128, and some device reaches it. `segment_ids`: the rows of device i along dp hold its images whole, slot after slot, each row carrying the id 8 * i + slot of its image, then -1 on the rows left. A device in the upper half of dp holds more rows than the device half the axis away. On each device the images that end after its row 96 cover at most 64 rows. Those rows plus all the rows of the device half the axis away come to at most 96. Both bounds are reached.
All inputs are finite; a program needn't handle non-finite values.
Results may differ from the reference program's by a relative error of at most 0.012.
The reference program's roundings to bfloat16 on the way (of `embedded`, `normed`, `weights`, `out_grad`, `value_grad` and `score_grad`) count: a program that leaves them out, or rounds other values in their place, can miss the bound.
Values may be sent and summed in bfloat16 or wider, within the bound.
A program may use at most 128 MiB of HBM per device.

```python
import math
import jax
import jax.numpy as jnp
from jax import lax

D = 6144
HEADS = 24
HD = 128
P_SIZE = 588
UNIT = 16
IMGS = 8
CAP = 128
ROWS = 1024
N_DP = 8


def split_units(totals, upper_draws):
    remain = totals
    portions = []
    for column in range(3):
        portion = jnp.minimum(remain, upper_draws[:, column])
        portions.append(portion)
        remain = remain - portion
    portions.append(remain)
    return jnp.stack(portions, axis=1)


def image_layout(key):
    pair_count = N_DP // 2
    base_key = jax.random.fold_in(key, 4242)
    tail_key, head_key, light_key, head_split, tail_split, light_split = jax.random.split(base_key, 6)
    tail_units = jax.random.randint(tail_key, (pair_count,), 2, 5)
    head_units = jnp.minimum(jax.random.randint(head_key, (pair_count,), 4, 6), 8 - tail_units)
    light_units = jax.random.randint(light_key, (pair_count,), 0, 7 - tail_units)
    head_units = head_units.at[0].set(5).at[1].set(4)
    tail_units = tail_units.at[0].set(3).at[1].set(4)
    light_units = light_units.at[0].set(3).at[1].set(2)
    head_parts = split_units(head_units, jax.random.randint(head_split, (pair_count, 4), 1, 5))
    tail_draws = jax.random.randint(tail_split, (pair_count, 4), 1, 5).at[1, 0].set(4)
    tail_parts = split_units(tail_units, tail_draws)
    light_parts = split_units(light_units, jax.random.randint(light_split, (pair_count, 4), 1, 5))
    heavy_side = jnp.concatenate([head_parts, tail_parts], axis=1)
    lighter = jnp.concatenate([light_parts, jnp.zeros_like(light_parts)], axis=1)
    unit_table = jnp.concatenate([lighter, heavy_side], axis=0)
    counts = (unit_table * UNIT).astype(jnp.int32)
    cumulative = jnp.cumsum(counts, axis=1)
    row_load = cumulative[:, -1]
    row_index = jnp.arange(CAP, dtype=jnp.int32)
    slot_index = jnp.sum((cumulative[:, None, :] <= row_index[None, :, None]).astype(jnp.int32), axis=-1)
    device = jnp.arange(N_DP, dtype=jnp.int32)[:, None]
    segment = jnp.where(row_index[None, :] < row_load[:, None], device * IMGS + slot_index, -1)
    return (counts.reshape(-1), segment.reshape(-1).astype(jnp.int32))


def draw_patch_counts(key, part):
    return image_layout(key)[0]


def draw_segment_ids(key, part):
    return image_layout(key)[1]


def level_of(stream_key, shape, pieces, smallest, high):
    level = 1.0
    for dim, shards_of in pieces:
        steps = jax.random.uniform(jax.random.fold_in(jax.random.fold_in(stream_key, 6), dim), (shards_of,), jnp.float32, smallest / len(pieces), high / len(pieces))
        level = level * jnp.repeat(jnp.exp(steps), shape[dim] // shards_of).reshape((-1,) + (1,) * (len(shape) - 1 - dim))
    return level


def normal_values(rng, extent, scale, limit, pieces=(), kind=jnp.bfloat16):
    loudness = level_of(rng, extent, pieces, -0.22, 0.18) if pieces else 1.0
    array = jax.random.normal(rng, extent, jnp.float32) * scale * loudness
    return jnp.minimum(jnp.maximum(array, -limit), limit).astype(kind)


def setup_inputs(seed: int = 0) -> dict:
    key_of = jax.random.split(jax.random.key(seed), 7)
    patches = normal_values(key_of[0], (ROWS, P_SIZE), 1.0, 6.0, ((0, 8),))
    embed_weight = normal_values(key_of[1], (D, P_SIZE), P_SIZE ** -0.5, 0.25, ((0, 32),))
    project_weight = normal_values(key_of[2], (D, 3, HEADS * HD), D ** -0.5, 0.078125, ((0, 8), (2, 4)))
    patch_counts = draw_patch_counts(jax.random.fold_in(key_of[6], 71), 0)
    segment_ids = draw_segment_ids(jax.random.fold_in(key_of[6], 71), 0)
    targets = normal_values(key_of[5], (ROWS, HEADS * HD), 0.5, 4.0, ((0, 8), (1, 4)))
    return dict(patches=patches, embed_weight=embed_weight, project_weight=project_weight, patch_counts=patch_counts, segment_ids=segment_ids, targets=targets)


def layer_norm(values):
    center = values - lax.optimization_barrier(jnp.mean(values, axis=-1, keepdims=True))
    spread = lax.optimization_barrier(jnp.mean(center * center, axis=-1, keepdims=True))
    return center * lax.rsqrt(spread + 1e-06)

def norm_grad(values, cotangent):
    return jax.vjp(layer_norm, values)[1](cotangent)[0]

def attend_block(query_raw, key_raw, value_rows, segment, target):
    inverse_root = 1.0 / math.sqrt(HD)
    query_normed = layer_norm(query_raw).astype(jnp.bfloat16)
    key_normed = layer_norm(key_raw).astype(jnp.bfloat16)
    scores = jnp.einsum('qhd,khd->hqk', query_normed.astype(jnp.float32), key_normed.astype(jnp.float32)) * inverse_root
    valid = segment >= 0
    allowed = (segment[:, None] == segment[None, :]) & valid[:, None]
    exponent = jnp.where(allowed[None], jnp.exp(scores), 0.0)
    denominator = lax.optimization_barrier(jnp.sum(exponent, axis=-1, keepdims=True))
    denominator = jnp.where(valid[None, :, None], denominator, 1.0)
    weights = (exponent / denominator).astype(jnp.bfloat16)
    attended = jnp.einsum('hqk,khd->qhd', weights.astype(jnp.float32), value_rows.astype(jnp.float32))
    feature_count = attended.shape[1] * attended.shape[2]
    error_rows = jnp.where(valid[:, None], attended.reshape(-1, feature_count) - target.astype(jnp.float32), 0.0)
    squared_sum = jnp.sum(error_rows * error_rows)
    return (query_normed, key_normed, weights, error_rows, squared_sum)

def attend_back(query_raw, key_raw, query_normed, key_normed, value_rows, weights, error_rows, patch_total):
    inverse_root = 1.0 / math.sqrt(HD)
    out_grad = (error_rows / patch_total).astype(jnp.bfloat16).reshape(query_normed.shape)
    prob_grad = jnp.einsum('qhd,khd->hqk', out_grad.astype(jnp.float32), value_rows.astype(jnp.float32))
    value_grad = jnp.einsum('hqk,qhd->khd', weights.astype(jnp.float32), out_grad.astype(jnp.float32)).astype(jnp.bfloat16)
    weight_float = weights.astype(jnp.float32)
    score_grad = (weight_float * (prob_grad - lax.optimization_barrier(jnp.sum(prob_grad * weight_float, axis=-1, keepdims=True))) * inverse_root).astype(jnp.bfloat16)
    normed_grad_q = jnp.einsum('hqk,khd->qhd', score_grad.astype(jnp.float32), key_normed.astype(jnp.float32))
    normed_grad_k = jnp.einsum('hqk,qhd->khd', score_grad.astype(jnp.float32), query_normed.astype(jnp.float32))
    query_grad = norm_grad(query_raw, normed_grad_q).astype(jnp.bfloat16)
    key_grad = norm_grad(key_raw, normed_grad_k).astype(jnp.bfloat16)
    return jnp.stack([query_grad, key_grad, value_grad], axis=1)

def reference(patches, embed_weight, project_weight, patch_counts, segment_ids, targets):
    embedded = jnp.dot(patches, embed_weight.T, preferred_element_type=jnp.float32).astype(jnp.bfloat16)
    normed = layer_norm(embedded.astype(jnp.float32)).astype(jnp.bfloat16)
    flat_weight = project_weight.reshape(D, 3 * HEADS * HD)
    projected = jnp.dot(normed, flat_weight, preferred_element_type=jnp.float32).reshape(N_DP, CAP, 3, HEADS, HD)
    patch_total = jnp.sum(patch_counts).astype(jnp.float32)
    segments = segment_ids.reshape(N_DP, CAP)
    target_blocks = targets.reshape(N_DP, CAP, HEADS * HD)

    def per_device(block_item):
        block_data, segment, target = block_item
        query_raw = block_data[:, 0]
        key_raw = block_data[:, 1]
        value_rows = block_data[:, 2].astype(jnp.bfloat16)
        query_normed, key_normed, weights, error_rows, squared_sum = attend_block(query_raw, key_raw, value_rows, segment, target)
        row_grads = attend_back(query_raw, key_raw, query_normed, key_normed, value_rows, weights, error_rows, patch_total)
        return (row_grads, squared_sum)
    row_grads, squared_sums = lax.map(per_device, (projected, segments, target_blocks))
    loss_value = jnp.sum(squared_sums) / (2.0 * patch_total)
    grad_rows = row_grads.reshape(N_DP * CAP, 3 * HEADS * HD)
    project_grad = jnp.dot(normed.T, grad_rows, preferred_element_type=jnp.float32).reshape(D, 3, HEADS * HD)
    return (project_grad, loss_value)
```

```python
import functools
import math

import jax
import jax.numpy as jnp
from jax import lax
from jax.experimental import pallas as pl
from jax.experimental.pallas import tpu as pltpu
from jax.sharding import PartitionSpec as P

HD = 128
MESH = pl.DeviceIdType.MESH
VMEM_BYTES = 62 * 1024 * 1024
F32, BF16 = jnp.float32, jnp.bfloat16


def remote(src, dst, send_sem, recv_sem, device_id):
    return pltpu.make_async_remote_copy(
        src_ref=src, dst_ref=dst, send_sem=send_sem, recv_sem=recv_sem,
        device_id=device_id, device_id_type=MESH,
    )


def greet(n, n_mp, d, m):
    barrier = pltpu.get_barrier_semaphore()
    for i in range(1, n):
        pl.semaphore_signal(barrier, inc=1, device_id={"dp": lax.rem(d + i, n)}, device_id_type=MESH)
    for i in range(1, n_mp):
        pl.semaphore_signal(barrier, inc=1, device_id={"mp": lax.rem(m + i, n_mp)}, device_id_type=MESH)
    pl.semaphore_wait(barrier, n - 1 + n_mp - 1)


def grid_side(nc):
    side = math.isqrt(nc)
    assert side * side == nc
    return side


def fdot(a, b, dims=((1,), (0,))):
    return lax.dot_general(a, b, (dims, ((), ())), preferred_element_type=F32)


def layer_parts(x):
    center = x - jnp.mean(x, axis=-1, keepdims=True)
    scale = lax.rsqrt(jnp.mean(center * center, axis=-1, keepdims=True) + 1e-06)
    return center * scale, scale


def norm_grad(unit, scale, g):
    along = jnp.mean(g * unit, axis=-1, keepdims=True)
    return scale * (g - jnp.mean(g, axis=-1, keepdims=True) - unit * along)


def block_kernel(
    n, n_mp, zc, hp,
    patches, embed, weight, counts, targets,
    out, loss,
    pall, zbuf, wp, wbuf, xt, e, nto, nrm, stats, metas, town, ttail, tgt,
    allow, live, pf, sb, r1, s2b, raw, r2, gath, stage, sq, zsq, psq, mine,
    w_sem, wx, wy, ms, mr, ps, pr, us, ur, vs, vr, es, er, el, fs, fr, ts, tr, tl,
    ss, sr, ns, nr, as_, ar, bs, br, gs, gr, hs, hr, cs, cr, zs, zr, qs, qr, os,
):
    d, m = lax.axis_index("dp"), lax.axis_index("mp")
    core, chip = lax.rem(d, 2), d // 2
    partner = d + 1 - 2 * core
    nc = n // 2
    side = grid_side(nc)
    cx, cy = lax.rem(chip, side), chip // side
    rows = targets.shape[0]
    keep = rows * 3 // 4
    low = rows - keep
    group = nc * keep
    piece = embed.shape[0]
    part = piece // zc
    block = n_mp * piece
    span = n // (2 * n_mp)
    imgs = counts.shape[0]
    chunks = pf.shape[0]
    wide = hp * HD
    pair = lax.rem(d + n // 2, n)
    is_low = jnp.where(d < n // 2, 1, 0)

    def chip_at(h, u, v):
        dx = u * (1 - h) + v * h
        dy = u * h + v * (1 - h)
        return lax.rem(cy + dy + side, side) * side + lax.rem(cx + dx + side, side)

    def dev(c):
        return {"dp": 2 * c + core}

    w_own = pltpu.make_async_copy(weight, wbuf.at[core], w_sem)
    w_own.start()
    t_own = pltpu.make_async_copy(targets, town, tl)
    t_own.start()
    p_local = pltpu.make_async_copy(patches, pall.at[chip], ps.at[0, 0])
    p_local.start()
    cum = jnp.zeros((imgs, 128), jnp.int32)
    line = lax.broadcasted_iota(jnp.int32, (imgs, 128), 0)
    total = jnp.int32(0)
    for s in range(imgs):
        total = total + counts[s]
        cum = jnp.where(line == s, total, cum)
    metas[d] = cum

    greet(n, n_mp, d, m)

    def p_first(u):
        return remote(patches, pall.at[chip], ps.at[u, 0], pr.at[u, 0], dev(chip_at(core, u, 0)))

    def p_second(u, v):
        at = chip_at(core, -u, 0)
        src = patches if u == 0 else pall.at[at]
        return remote(src, pall.at[at], ps.at[u, v], pr.at[u, v], dev(chip_at(core, 0, v)))

    def m_copy(i):
        return remote(metas.at[d], metas.at[d], ms.at[i], mr.at[i], {"dp": lax.rem(d + i, n)})

    for u in range(1, side):
        p_first(u).start()
    for v in range(1, side):
        p_second(0, v).start()

    def z_copy(up, i, c):
        origin = m - i if up else m + i
        src = embed.at[pl.ds(c * part, part)] if i == 0 else zbuf.at[origin, c]
        send, recv = (us, ur) if up else (vs, vr)
        return remote(src, zbuf.at[origin, c], send.at[i, c], recv.at[i + 1, c], {"mp": m + 1 if up else m - 1})

    def z_wait(up, i, c):
        origin = m - i if up else m + i
        send, recv = (us, ur) if up else (vs, vr)
        remote(zbuf.at[origin, c], zbuf.at[origin, c], send.at[i, c], recv.at[i, c], {"mp": m - 1 if up else m + 1}).wait_recv()

    def z_has(up, i):
        return m - i >= 0 if up else m + i <= n_mp - 1

    def z_sends(up, i):
        return (m - i >= 0) & (m < n_mp - 1) if up else (m + i <= n_mp - 1) & (m > 0)

    slot = lax.rem(d, 2 * n_mp)
    rel_own = lax.rem(chip, n_mp)

    def owner(origin):
        return origin * span + d // (2 * n_mp)

    def e_copy(origin, src, c):
        return remote(src, wp.at[slot, c], es.at[origin, c], er.at[rel_own, c], dev(owner(origin)))

    def e_local(src, c):
        return pltpu.make_async_copy(src, wp.at[slot, c], el.at[c])

    def e_start(origin, own, c):
        src = embed.at[pl.ds(c * part, part)] if own else zbuf.at[origin, c]

        @pl.when(owner(origin) != chip)
        def _():
            e_copy(origin, src, c).start()

        @pl.when(owner(origin) == chip)
        def _():
            e_local(src, c).start()

    for c in range(zc):
        for up in (True, False):
            @pl.when(z_sends(up, 0))
            def _():
                z_copy(up, 0, c).start()
    for c in range(zc):
        e_start(m, True, c)
    for i in range(1, n):
        m_copy(i).start()

    w_swap = remote(weight, wbuf.at[core], wx, wy, {"dp": partner})
    w_swap.start()

    p_local.wait()
    for u in range(1, side):
        p_first(u).wait_recv()
        for v in range(1, side):
            p_second(u, v).start()

    def t_copy():
        return remote(town.at[pl.ds(low, keep)], ttail, ts, tr, {"dp": pair})

    t_own.wait()

    @pl.when(is_low == 0)
    def _():
        t_copy().start()

    @pl.when(is_low == 1)
    def _():
        sq[...] = jnp.zeros_like(sq)

    @pl.when(is_low == 0)
    def _():
        sq[...] = jnp.zeros_like(sq)
        ttail[...] = jnp.zeros_like(ttail)

    def z_step(i):
        for c in range(zc):
            for up in (True, False):
                @pl.when(z_has(up, i))
                def _():
                    z_wait(up, i, c)
                    if i < n_mp - 1:
                        @pl.when(z_sends(up, i))
                        def _():
                            z_copy(up, i, c).start()
                    e_start(m - i if up else m + i, False, c)

    z_step(1)

    for v in range(1, side):
        for u in range(side):
            p_second(u, v).wait_recv()
    for i in range(1, n):
        m_copy(i).wait_recv()

    def ends(meta):
        fits = jnp.zeros((1, 1), jnp.int32)
        for s in range(imgs):
            at = meta[s:s + 1, 0:1]
            fits = jnp.maximum(fits, jnp.where(at <= keep, at, 0))
        return fits, meta[imgs - 1:imgs, 0:1]

    lane = lax.broadcasted_iota(jnp.int32, (1, group), 1)
    source = jnp.full((1, group), -1, jnp.int32)
    for j in range(nc // 2):
        far = j + nc // 2
        _, held = ends(metas[2 * j + core])
        fits, full = ends(metas[2 * far + core])
        r = lane - j * keep
        tail = fits + r - held
        at = jnp.where(r < held, j * rows + r, jnp.where(tail < full, far * rows + tail, -1))
        source = jnp.where((r >= 0) & (r < keep), at, source)
        r = lane - far * keep
        source = jnp.where((r >= 0) & (r < fits) & (r < keep), far * rows + r, source)
    xt[...] = jnp.zeros_like(xt)
    picked = None
    for j in range(nc):
        spot = lax.broadcasted_iota(jnp.int32, (rows, group), 0) + j * rows
        pick = jnp.where(spot == source, 1.0, 0.0).astype(BF16)
        term = fdot(pall[j], pick)
        picked = term if picked is None else picked + term
    xt[...] = picked.astype(BF16)

    fits_own, full_own = ends(metas[d])
    fits_far, full_far = ends(metas[pair])
    limit = is_low * full_own + (1 - is_low) * fits_own

    def place(shape, dim):
        r = lax.broadcasted_iota(jnp.int32, shape, dim)
        tail = fits_far + r - limit
        near = r < limit
        moved = (r >= limit) & (tail < full_far) & (is_low == 1)
        return r, tail, near, moved

    def ident(shape, dim):
        r, tail, near, moved = place(shape, dim)
        first = jnp.zeros(shape, jnp.int32)
        second = jnp.full(shape, imgs, jnp.int32)
        mine_, theirs = metas[d], metas[pair]
        for s in range(imgs):
            first = first + jnp.where(mine_[s:s + 1, 0:1] <= r, 1, 0)
            second = second + jnp.where(theirs[s:s + 1, 0:1] <= tail, 1, 0)
        return jnp.where(near, first, jnp.where(moved, second, -1))

    of_row, of_col = ident((keep, keep), 0), ident((keep, keep), 1)
    allow[...] = jnp.where((of_row == of_col) & (of_row >= 0), 1.0, 0.0)
    live[...] = jnp.where(ident((keep, HD), 0) >= 0, 1.0, 0.0)
    total_f = jnp.zeros((1, 1), jnp.int32)
    for i in range(n):
        total_f = total_f + metas[i][imgs - 1:imgs, 0:1]
    total_f = total_f.astype(F32)

    for i in range(2, n_mp):
        z_step(i)

    @pl.when(is_low == 1)
    def _():
        t_copy().wait_recv()

    r, tail, near, moved = place((keep, rows), 0)
    col = lax.broadcasted_iota(jnp.int32, (keep, rows), 1)
    pick_own = jnp.where(near & (col == r), 1.0, 0.0).astype(BF16)
    r, tail, near, moved = place((keep, keep), 0)
    col = lax.broadcasted_iota(jnp.int32, (keep, keep), 1)
    pick_far = jnp.where(moved & (col == tail - low), 1.0, 0.0).astype(BF16)
    tgt[...] = fdot(pick_own, town[...]) + fdot(pick_far, ttail[...])

    base = n_mp * lax.rem(chip, span)

    def f_copy(i, c):
        q = 2 * i + core
        return remote(wp.at[q, c], wp.at[q, c], fs.at[i, c], fr.at[i, c], {"dp": partner})

    for c in range(zc):
        for i in range(n_mp):
            @pl.when(base + i == chip)
            def _():
                e_local(zbuf.at[0, c], c).wait()

            @pl.when(base + i != chip)
            def _():
                q = 2 * i + core
                remote(wp.at[q, c], wp.at[q, c], es.at[i, c], er.at[i, c], {"dp": partner}).wait_recv()

            f_copy(i, c).start()

    means, squares = [], []
    for i in range(n_mp):
        for c in range(zc):
            f_copy(i, c).wait_recv()
        both = jnp.concatenate([wp[2 * i + k, c] for k in range(2) for c in range(zc)], axis=0)
        value = fdot(both, xt[...]).astype(BF16)
        b, at = divmod(2 * i * piece, block)
        e[b, at:at + 2 * piece, :] = value
        value = value.astype(F32)
        mean = jnp.mean(value, axis=0, keepdims=True)
        center = value - mean
        means.append(mean)
        squares.append(jnp.sum(center * center, axis=0, keepdims=True))
    mean = sum(means) * (1.0 / n_mp)
    square = sum(squares)
    for one in means:
        square = square + (2.0 * piece) * ((one - mean) * (one - mean))
    stats[0, 0:1, :] = mean
    stats[0, 1:2, :] = square

    def s_copy(i):
        return remote(stats.at[0], stats.at[i], ss.at[i], sr.at[i], dev(lax.rem(chip + i, nc)))

    for i in range(1, nc):
        s_copy(i).start()
    w_own.wait()
    w_swap.wait_recv()
    for i in range(1, nc):
        s_copy(i).wait_recv()
    mean = sum(stats[i, 0:1, :] for i in range(nc)) * (1.0 / nc)
    square = jnp.zeros((1, group), F32)
    for i in range(nc):
        gap = stats[i, 0:1, :] - mean
        square = square + stats[i, 1:2, :] + (2.0 * block) * (gap * gap)
    scale = lax.rsqrt(square * (1.0 / (2.0 * block * nc)) + 1e-06)
    step = 384 if block % 384 == 0 else block
    for b in range(2):
        for at in range(0, block, step):
            value = (e[b, at:at + step, :].astype(F32) - mean) * scale
            value = value.astype(BF16)
            e[b, at:at + step, :] = value
            nrm[b, :, at:at + step] = value.T

    def way(k):
        return lax.rem(k + core, 2)

    def a_copy(k, u):
        return remote(sb.at[k, u], r1.at[k, u], as_.at[k, u], ar.at[k, u], dev(chip_at(way(k), u, 0)))

    def b_copy(k, v):
        return remote(s2b.at[k, v], r2.at[k, v], bs.at[k, v], br.at[k, v], dev(chip_at(way(k), 0, v)))

    def project(k, carry):
        acc = None
        for b in range(2):
            cols = jnp.concatenate(
                [wbuf[b, s, :, pl.ds(pl.multiple_of(k * wide, wide), wide)] for s in range(3)], axis=1
            )
            term = fdot(nrm[b], cols)
            acc = term if acc is None else acc + term
        pf[k] = acc.reshape(nc, keep, 3 * wide)
        for u in range(1, side):
            for v in range(side):
                sb[k, u, v] = pf[k, chip_at(way(k), u, v)].astype(BF16)
            a_copy(k, u).start()
        return carry

    lax.fori_loop(0, chunks, project, 0)

    n_copy = remote(e.at[1 - core], nto, ns, nr, {"dp": partner})
    n_copy.start()

    def fold(k, carry):
        for u in range(1, side):
            a_copy(k, u).wait_recv()
        for v in range(1, side):
            value = pf[k, chip_at(way(k), 0, v)]
            for u in range(1, side):
                value = value + r1[k, u, v].astype(F32)
            s2b[k, v] = value.astype(BF16)
            b_copy(k, v).start()
        value = pf[k, chip]
        for u in range(1, side):
            value = value + r1[k, u, 0].astype(F32)
        raw[k] = value
        return carry

    lax.fori_loop(0, chunks, fold, 0)

    root = 1.0 / math.sqrt(HD)
    per_total = 1.0 / total_f

    def g_first(k, u):
        return remote(gath.at[k, 0, chip], gath.at[k, 0, chip], gs.at[k, u], gr.at[k, u], dev(chip_at(way(k), u, 0)))

    def g_second(k, u, v):
        at = chip_at(way(k), -u, 0)
        return remote(gath.at[k, 0, at], gath.at[k, 0, at], hs.at[k, u, v], hr.at[k, u, v], dev(chip_at(way(k), 0, v)))

    def g_across(k, u, v):
        at = chip_at(way(k), -u, -v)
        return remote(gath.at[k, 0, at], gath.at[k, 1, at], cs.at[k, u, v], cr.at[k, u, v], {"dp": partner})

    def attend(k):
        for v in range(1, side):
            b_copy(k, v).wait_recv()
        mask, alive = allow[...], live[...]
        error_sum = jnp.zeros((8, HD), F32)
        for h in range(hp):
            part_of = []
            for s in range(3):
                cols = slice(s * wide + h * HD, s * wide + (h + 1) * HD)
                value = raw[k, :, cols]
                for v in range(1, side):
                    value = value + r2[k, v, :, cols].astype(F32)
                part_of.append(value)
            q_unit, q_scale = layer_parts(part_of[0])
            k_unit, k_scale = layer_parts(part_of[1])
            q_n, k_n, v_n = q_unit.astype(BF16), k_unit.astype(BF16), part_of[2].astype(BF16)
            scores = fdot(q_n, k_n, ((1,), (1,))) * root
            power = jnp.where(mask > 0.0, jnp.exp(scores), 0.0)
            below = jnp.sum(power, axis=-1, keepdims=True)
            below = jnp.where(below > 0.0, below, 1.0)
            weights = (power / below).astype(BF16)
            want = tgt[:, pl.ds(pl.multiple_of(k * wide + h * HD, HD), HD)]
            error = jnp.where(alive > 0.0, fdot(weights, v_n) - want, 0.0)
            error_sum = error_sum + jnp.sum((error * error).reshape(keep // 8, 8, HD), axis=0)
            out_grad = (error * per_total).astype(BF16)
            prob_grad = fdot(out_grad, v_n, ((1,), (1,)))
            value_grad = fdot(weights, out_grad, ((0,), (0,)))
            weight_f = weights.astype(F32)
            score_grad = (
                weight_f * (prob_grad - jnp.sum(prob_grad * weight_f, axis=-1, keepdims=True)) * root
            ).astype(BF16)
            q_grad = norm_grad(q_unit, q_scale, fdot(score_grad, k_n))
            k_grad = norm_grad(k_unit, k_scale, fdot(score_grad, q_n, ((0,), (0,))))
            for s, value in enumerate((q_grad, k_grad, value_grad)):
                gath[k, 0, chip, :, s * wide + h * HD:s * wide + (h + 1) * HD] = value.astype(BF16)
        sq[...] += error_sum
        for u in range(1, side):
            g_first(k, u).start()
        for v in range(1, side):
            g_second(k, 0, v).start()
        g_across(k, 0, 0).start()

    def relay(k):
        for u in range(1, side):
            g_first(k, u).wait_recv()
            for v in range(1, side):
                g_second(k, u, v).start()
            g_across(k, u, 0).start()

    def cross(k):
        for u in range(side):
            for v in range(1, side):
                g_second(k, u, v).wait_recv()
                g_across(k, u, v).start()

    def o_copy(k):
        cols = pl.ds(pl.multiple_of(k * wide, wide), wide)
        return pltpu.make_async_copy(stage.at[k], out.at[:, :, cols], os.at[k])

    def finish(k):
        for u in range(side):
            for v in range(side):
                g_across(k, u, v).wait_recv()
        right = gath[k].reshape(2 * group, 3 * wide)
        left = jnp.concatenate([e[core], nto[...]], axis=1)
        value = fdot(left, right)
        for s in range(3):
            stage[k, s] = value[:, s * wide:(s + 1) * wide]
        o_copy(k).start()

    n_copy.wait_recv()

    def flow(i, carry):
        @pl.when(i < chunks)
        def _():
            attend(i)

        @pl.when((i >= 1) & (i <= chunks))
        def _():
            relay(i - 1)

        @pl.when((i >= 2) & (i <= chunks + 1))
        def _():
            cross(i - 2)

        @pl.when(i >= 3)
        def _():
            finish(i - 3)

        return carry

    lax.fori_loop(0, chunks + 2, flow, 0)

    def y_copy(i):
        return remote(sq, zsq.at[i], zs.at[i], zr.at[i], {"mp": lax.rem(m + i, n_mp)})

    def l_copy(i):
        return remote(mine, psq.at[i], qs.at[i], qr.at[i], {"dp": lax.rem(d + i, n)})

    for i in range(1, n_mp):
        y_copy(i).start()
    value = sq[...]
    for i in range(1, n_mp):
        y_copy(i).wait_recv()
        value = value + zsq[i]
    mine[...] = value
    for i in range(1, n):
        l_copy(i).start()
    finish(chunks - 1)
    for i in range(1, n):
        l_copy(i).wait_recv()
        value = value + psq[i]
    value = jnp.sum(jnp.sum(value, axis=1, keepdims=True), axis=0, keepdims=True)
    loss[...] = jnp.broadcast_to(value * (0.5 * per_total), loss.shape)

    for u in range(1, side):
        p_first(u).wait_send()
    for v in range(1, side):
        for u in range(side):
            p_second(u, v).wait_send()
    for i in range(1, n):
        m_copy(i).wait_send()
        l_copy(i).wait_send()
    for i in range(1, n_mp):
        y_copy(i).wait_send()
    for c in range(zc):
        for i in range(n_mp - 1):
            for up in (True, False):
                @pl.when(z_sends(up, i))
                def _():
                    z_copy(up, i, c).wait_send()
        for i in range(n_mp):
            f_copy(i, c).wait_send()

            @pl.when(owner(i) != chip)
            def _():
                e_copy(i, zbuf.at[i, c], c).wait_send()

    @pl.when(is_low == 0)
    def _():
        t_copy().wait_send()

    w_swap.wait_send()
    n_copy.wait_send()
    for i in range(1, nc):
        s_copy(i).wait_send()

    def drain(k, carry):
        for u in range(1, side):
            a_copy(k, u).wait_send()
            g_first(k, u).wait_send()
        for v in range(1, side):
            b_copy(k, v).wait_send()
            for u in range(side):
                g_second(k, u, v).wait_send()
        for u in range(side):
            for v in range(side):
                g_across(k, u, v).wait_send()
        o_copy(k).wait()
        return carry

    lax.fori_loop(0, chunks, drain, 0)


def run_block(patches, embed, weight, counts, targets, n, n_mp):
    length, rows = patches.shape
    piece = embed.shape[0]
    columns = weight.shape[2]
    heads = columns // HD
    nc = n // 2
    side = grid_side(nc)
    keep = rows * 3 // 4
    group = nc * keep
    block = n_mp * piece
    imgs = counts.shape[0]
    assert n % (2 * n_mp) == 0 and block == weight.shape[1]
    zc = 2 if piece % 32 == 0 else 1
    hp = 2 if heads % 2 == 0 else 1
    chunks = heads // hp
    wide = 3 * hp * HD
    dma = lambda *k: pltpu.SemaphoreType.DMA(k) if k else pltpu.SemaphoreType.DMA
    anywhere = pl.BlockSpec(memory_space=pl.ANY)
    vmem = pl.BlockSpec(memory_space=pltpu.VMEM)
    v = pltpu.VMEM
    return pl.pallas_call(
        functools.partial(block_kernel, n, n_mp, zc, hp),
        out_shape=(
            jax.ShapeDtypeStruct((3, block, columns), F32),
            jax.ShapeDtypeStruct((8, 128), F32),
        ),
        in_specs=[anywhere, anywhere, anywhere, pl.BlockSpec(memory_space=pltpu.SMEM), anywhere],
        out_specs=(anywhere, vmem),
        scratch_shapes=[
            v((nc, length, rows), BF16),
            v((n_mp, zc, piece // zc, length), BF16),
            v((2 * n_mp, zc, piece // zc, length), BF16),
            v((2,) + weight.shape, BF16),
            v((length, group), BF16),
            v((2, block, group), BF16),
            v((block, group), BF16),
            v((2, group, block), BF16),
            v((nc, 8, group), F32),
            v((n, imgs, 128), jnp.int32),
            v((rows, columns), BF16),
            v((keep, columns), BF16),
            v((keep, columns), F32),
            v((keep, keep), F32),
            v((keep, HD), F32),
            v((chunks, nc, keep, wide), F32),
            v((chunks, side, side, keep, wide), BF16),
            v((chunks, side, side, keep, wide), BF16),
            v((chunks, side, keep, wide), BF16),
            v((chunks, keep, wide), F32),
            v((chunks, side, keep, wide), BF16),
            v((chunks, 2, nc, keep, wide), BF16),
            v((chunks, 3, block, hp * HD), F32),
            v((8, 128), F32),
            v((n_mp, 8, 128), F32),
            v((n, 8, 128), F32),
            v((8, 128), F32),
            dma(), dma(), dma(),
            dma(n), dma(n),
            dma(side, side), dma(side, side),
            dma(n_mp, zc), dma(n_mp, zc), dma(n_mp, zc), dma(n_mp, zc),
            dma(n_mp, zc), dma(n_mp, zc), dma(zc),
            dma(n_mp, zc), dma(n_mp, zc),
            dma(), dma(), dma(),
            dma(nc), dma(nc),
            dma(), dma(),
            dma(chunks, side), dma(chunks, side),
            dma(chunks, side), dma(chunks, side),
            dma(chunks, side), dma(chunks, side),
            dma(chunks, side, side), dma(chunks, side, side),
            dma(chunks, side, side), dma(chunks, side, side),
            dma(n_mp), dma(n_mp), dma(n), dma(n),
            dma(chunks),
        ],
        compiler_params=pltpu.CompilerParams(
            collective_id=0, has_side_effects=True, vmem_limit_bytes=VMEM_BYTES
        ),
    )(patches, embed, weight, counts, targets)


def local(n, n_mp, patches, embed_weight, project_weight, patch_counts, segment_ids, targets):
    del segment_ids
    weight_grad, loss = run_block(
        patches.T, embed_weight, jnp.transpose(project_weight, (1, 0, 2)), patch_counts, targets, n, n_mp
    )
    return (jnp.transpose(weight_grad, (1, 0, 2)), loss[0, 0])


def solution(mesh):
    in_specs = (
        P("dp", None),
        P(("mp", "dp"), None),
        P("dp", None, "mp"),
        P("dp"),
        P("dp"),
        P("dp", "mp"),
    )
    out_specs = (P("dp", None, "mp"), P())
    return jax.shard_map(
        functools.partial(local, mesh.shape["dp"], mesh.shape["mp"]), mesh=mesh, in_specs=in_specs, out_specs=out_specs, check_vma=False)
```

```python
import functools
import math

import jax
import jax.numpy as jnp
from jax import lax
from jax.experimental import pallas as pl
from jax.experimental.pallas import tpu as pltpu
from jax.sharding import PartitionSpec as P

HD = 128
MESH = pl.DeviceIdType.MESH
VMEM_BYTES = 62 * 1024 * 1024
F32, BF16 = jnp.float32, jnp.bfloat16


def remote(src, dst, send_sem, recv_sem, device_id):
    return pltpu.make_async_remote_copy(
        src_ref=src, dst_ref=dst, send_sem=send_sem, recv_sem=recv_sem,
        device_id=device_id, device_id_type=MESH,
    )


def greet(n, n_mp, d, m):
    barrier = pltpu.get_barrier_semaphore()
    for i in range(1, n):
        pl.semaphore_signal(barrier, inc=1, device_id={"dp": lax.rem(d + i, n)}, device_id_type=MESH)
    for i in range(1, n_mp):
        pl.semaphore_signal(barrier, inc=1, device_id={"mp": lax.rem(m + i, n_mp)}, device_id_type=MESH)
    pl.semaphore_wait(barrier, n - 1 + n_mp - 1)


def grid_side(nc):
    side = math.isqrt(nc)
    assert side * side == nc
    return side


def fdot(a, b, dims=((1,), (0,))):
    return lax.dot_general(a, b, (dims, ((), ())), preferred_element_type=F32)


def layer_parts(x):
    center = x - jnp.mean(x, axis=-1, keepdims=True)
    scale = lax.rsqrt(jnp.mean(center * center, axis=-1, keepdims=True) + 1e-06)
    return center * scale, scale


def norm_grad(unit, scale, g):
    along = jnp.mean(g * unit, axis=-1, keepdims=True)
    return scale * (g - jnp.mean(g, axis=-1, keepdims=True) - unit * along)


def block_kernel(
    n, n_mp, zc, hp,
    patches, embed, weight, counts, targets,
    out, loss,
    pall, zbuf, wp, wbuf, xt, xn, e, nto, nrm, center_of, of_row, sums, stats, metas, town, ttail, tgt,
    allow, live, pf, sb, r1, s2b, raw, r2, gath, stage, sq, zsq, psq, mine,
    w_sem, wx, wy, ms, mr, ps, pr, us, ur, vs, vr, es, er, el, fs, fr, ts, tr, tl,
    ss, sr, ks, kr, ns, nr, as_, ar, bs, br, gs, gr, hs, hr, cs, cr, zs, zr, qs, qr, os,
):
    d, m = lax.axis_index("dp"), lax.axis_index("mp")
    core, chip = lax.rem(d, 2), d // 2
    partner = d + 1 - 2 * core
    nc = n // 2
    side = grid_side(nc)
    cx, cy = lax.rem(chip, side), chip // side
    rows = targets.shape[0]
    keep = rows * 3 // 4
    low = rows - keep
    group = nc * keep
    piece = embed.shape[0]
    part = piece // zc
    block = n_mp * piece
    span = n // (2 * n_mp)
    imgs = counts.shape[0]
    chunks = pf.shape[0]
    wide = hp * HD
    pair = lax.rem(d + n // 2, n)
    is_low = jnp.where(d < n // 2, 1, 0)

    def chip_at(h, u, v):
        dx = u * (1 - h) + v * h
        dy = u * h + v * (1 - h)
        return lax.rem(cy + dy + side, side) * side + lax.rem(cx + dx + side, side)

    def dev(c):
        return {"dp": 2 * c + core}

    w_own = pltpu.make_async_copy(weight, wbuf.at[core], w_sem)
    w_own.start()
    t_own = pltpu.make_async_copy(targets, town, tl)
    t_own.start()
    p_local = pltpu.make_async_copy(patches, pall.at[chip], ps.at[0, 0])
    p_local.start()
    cum = jnp.zeros((imgs, 128), jnp.int32)
    line = lax.broadcasted_iota(jnp.int32, (imgs, 128), 0)
    total = jnp.int32(0)
    for s in range(imgs):
        total = total + counts[s]
        cum = jnp.where(line == s, total, cum)
    metas[d] = cum

    greet(n, n_mp, d, m)

    def p_first(u):
        return remote(patches, pall.at[chip], ps.at[u, 0], pr.at[u, 0], dev(chip_at(core, u, 0)))

    def p_second(u, v):
        at = chip_at(core, -u, 0)
        src = patches if u == 0 else pall.at[at]
        return remote(src, pall.at[at], ps.at[u, v], pr.at[u, v], dev(chip_at(core, 0, v)))

    def m_copy(i):
        return remote(metas.at[d], metas.at[d], ms.at[i], mr.at[i], {"dp": lax.rem(d + i, n)})

    for u in range(1, side):
        p_first(u).start()
    for v in range(1, side):
        p_second(0, v).start()

    def z_copy(up, i, c):
        origin = m - i if up else m + i
        src = embed.at[pl.ds(c * part, part)] if i == 0 else zbuf.at[origin, c]
        send, recv = (us, ur) if up else (vs, vr)
        return remote(src, zbuf.at[origin, c], send.at[i, c], recv.at[i + 1, c], {"mp": m + 1 if up else m - 1})

    def z_wait(up, i, c):
        origin = m - i if up else m + i
        send, recv = (us, ur) if up else (vs, vr)
        remote(zbuf.at[origin, c], zbuf.at[origin, c], send.at[i, c], recv.at[i, c], {"mp": m - 1 if up else m + 1}).wait_recv()

    def z_has(up, i):
        return m - i >= 0 if up else m + i <= n_mp - 1

    def z_sends(up, i):
        return (m - i >= 0) & (m < n_mp - 1) if up else (m + i <= n_mp - 1) & (m > 0)

    slot = lax.rem(d, 2 * n_mp)
    rel_own = lax.rem(chip, n_mp)

    def owner(origin):
        return origin * span + d // (2 * n_mp)

    def e_copy(origin, src, c):
        return remote(src, wp.at[slot, c], es.at[origin, c], er.at[rel_own, c], dev(owner(origin)))

    def e_local(src, c):
        return pltpu.make_async_copy(src, wp.at[slot, c], el.at[c])

    def e_start(origin, own, c):
        src = embed.at[pl.ds(c * part, part)] if own else zbuf.at[origin, c]

        @pl.when(owner(origin) != chip)
        def _():
            e_copy(origin, src, c).start()

        @pl.when(owner(origin) == chip)
        def _():
            e_local(src, c).start()

    def z_own(c):
        for up in (True, False):
            @pl.when(z_sends(up, 0))
            def _():
                z_copy(up, 0, c).start()
        e_start(m, True, c)

    for c in range(min(2, zc)):
        z_own(c)
    for i in range(1, n):
        m_copy(i).start()

    w_swap = remote(weight, wbuf.at[core], wx, wy, {"dp": partner})
    w_swap.start()

    p_local.wait()
    for u in range(1, side):
        p_first(u).wait_recv()
        for v in range(1, side):
            p_second(u, v).start()

    def t_copy():
        return remote(town.at[pl.ds(low, keep)], ttail, ts, tr, {"dp": pair})

    t_own.wait()

    @pl.when(is_low == 0)
    def _():
        t_copy().start()

    @pl.when(is_low == 1)
    def _():
        sq[...] = jnp.zeros_like(sq)

    @pl.when(is_low == 0)
    def _():
        sq[...] = jnp.zeros_like(sq)
        ttail[...] = jnp.zeros_like(ttail)

    def z_wave(w):
        for i in range(1, n_mp):
            c = w + 1 - i
            if 0 <= c < zc:
                for up in (True, False):
                    @pl.when(z_has(up, i))
                    def _():
                        z_wait(up, i, c)
                        if i < n_mp - 1:
                            @pl.when(z_sends(up, i))
                            def _():
                                z_copy(up, i, c).start()
                        e_start(m - i if up else m + i, False, c)
        if w + 2 < zc:
            z_own(w + 2)

    waves = zc + n_mp - 2
    for w in range(waves // 2):
        z_wave(w)

    for v in range(1, side):
        for u in range(side):
            p_second(u, v).wait_recv()
    for i in range(1, n):
        m_copy(i).wait_recv()

    def ends(meta):
        fits = jnp.zeros((1, 1), jnp.int32)
        for s in range(imgs):
            at = meta[s:s + 1, 0:1]
            fits = jnp.maximum(fits, jnp.where(at <= keep, at, 0))
        return fits, meta[imgs - 1:imgs, 0:1]

    lane = lax.broadcasted_iota(jnp.int32, (1, group), 1)
    source = jnp.full((1, group), -1, jnp.int32)
    for j in range(nc // 2):
        far = j + nc // 2
        _, held = ends(metas[2 * j + core])
        fits, full = ends(metas[2 * far + core])
        r = lane - j * keep
        tail = fits + r - held
        at = jnp.where(r < held, j * rows + r, jnp.where(tail < full, far * rows + tail, -1))
        source = jnp.where((r >= 0) & (r < keep), at, source)
        r = lane - far * keep
        source = jnp.where((r >= 0) & (r < fits) & (r < keep), far * rows + r, source)
    picked = None
    for j in range(nc):
        place_of = lax.broadcasted_iota(jnp.int32, (rows, group), 0) + j * rows
        pick = jnp.where(place_of == source, 1.0, 0.0).astype(BF16)
        term = fdot(pall[j], pick)
        picked = term if picked is None else picked + term
    xt[...] = picked.astype(BF16)
    xn[...] = picked.astype(BF16).T
    for b in range(2):
        nrm[b, group:group + 16, :] = jnp.ones((16, block), BF16)

    fits_own, full_own = ends(metas[d])
    fits_far, full_far = ends(metas[pair])
    limit = is_low * full_own + (1 - is_low) * fits_own

    def place(shape, dim):
        r = lax.broadcasted_iota(jnp.int32, shape, dim)
        tail = fits_far + r - limit
        near = r < limit
        moved = (r >= limit) & (tail < full_far) & (is_low == 1)
        return r, tail, near, moved

    def ident(shape, dim):
        r, tail, near, moved = place(shape, dim)
        first = jnp.zeros(shape, jnp.int32)
        second = jnp.full(shape, imgs, jnp.int32)
        mine_, theirs = metas[d], metas[pair]
        for s in range(imgs):
            first = first + jnp.where(mine_[s:s + 1, 0:1] <= r, 1, 0)
            second = second + jnp.where(theirs[s:s + 1, 0:1] <= tail, 1, 0)
        return jnp.where(near, first, jnp.where(moved, second, -1))

    down, over = ident((keep, keep), 0), ident((keep, keep), 1)
    allow[...] = jnp.where((down == over) & (down >= 0), 1.0, 0.0)
    live[...] = jnp.where(ident((keep, HD), 0) >= 0, 1.0, 0.0)
    total_f = jnp.zeros((1, 1), jnp.int32)
    for i in range(n):
        total_f = total_f + metas[i][imgs - 1:imgs, 0:1]
    total_f = total_f.astype(F32)

    for w in range(waves // 2, waves):
        z_wave(w)

    @pl.when(is_low == 1)
    def _():
        t_copy().wait_recv()

    r, tail, near, moved = place((keep, rows), 0)
    col = lax.broadcasted_iota(jnp.int32, (keep, rows), 1)
    pick_own = jnp.where(near & (col == r), 1.0, 0.0).astype(BF16)
    r, tail, near, moved = place((keep, keep), 0)
    col = lax.broadcasted_iota(jnp.int32, (keep, keep), 1)
    pick_far = jnp.where(moved & (col == tail - low), 1.0, 0.0).astype(BF16)
    tgt[...] = fdot(pick_own, town[...]) + fdot(pick_far, ttail[...])

    base = n_mp * lax.rem(chip, span)

    def f_copy(i, c):
        q = 2 * i + core
        return remote(wp.at[q, c], wp.at[q, c], fs.at[i, c], fr.at[i, c], {"dp": partner})

    for c in range(zc):
        for i in range(n_mp):
            @pl.when(base + i == chip)
            def _():
                e_local(zbuf.at[0, c], c).wait()

            @pl.when(base + i != chip)
            def _():
                q = 2 * i + core
                remote(wp.at[q, c], wp.at[q, c], es.at[i, c], er.at[i, c], {"dp": partner}).wait_recv()

            f_copy(i, c).start()

    per = 1 if 2 * piece % 128 == 0 else n_mp // 2
    lump = 2 * piece * per

    def pieces(i):
        return jnp.concatenate(
            [wp[2 * j + k, c] for j in range(i * per, (i + 1) * per) for k in range(2) for c in range(zc)], axis=0
        )

    def spot(i):
        return divmod(i * lump, block)

    for i in range(n_mp // per):
        for j in range(i * per, (i + 1) * per):
            for c in range(zc):
                f_copy(j, c).wait_recv()
        b, at = spot(i)
        nrm[b, 0:group, at:at + lump] = fdot(xn[...], pieces(i), ((1,), (1,))).astype(BF16)
    ones = jnp.ones((block, 128), BF16)
    about = (fdot(nrm[0, 0:group, :], ones) + fdot(nrm[1, 0:group, :], ones)) * (0.5 / block)
    center_of[...] = about
    w_own.wait()
    w_swap.wait_recv()

    def way(k):
        return lax.rem(k + core, 2)

    def a_copy(k, u):
        return remote(sb.at[k, u], r1.at[k, u], as_.at[k, u], ar.at[k, u], dev(chip_at(way(k), u, 0)))

    def b_copy(k, v):
        return remote(s2b.at[k, v], r2.at[k, v], bs.at[k, v], br.at[k, v], dev(chip_at(way(k), 0, v)))

    def project(k, carry):
        acc = None
        for b in range(2):
            cols = jnp.concatenate(
                [wbuf[b, s, :, pl.ds(pl.multiple_of(k * wide, wide), wide)] for s in range(3)], axis=1
            )
            term = fdot(nrm[b], cols)
            acc = term if acc is None else acc + term
        for s in range(3 * hp):
            sums[0, k, s:s + 1, :] = acc[group:group + 1, s * HD:(s + 1) * HD]
        center = jnp.concatenate([center_of[...]] * (3 * hp), axis=1)
        pf[k] = (acc[0:group] - center * acc[group:group + 1]).reshape(nc, keep, 3 * wide)
        for u in range(1, side):
            for v in range(side):
                sb[k, u, v] = pf[k, chip_at(way(k), u, v)].astype(BF16)
            a_copy(k, u).start()
        return carry

    lax.fori_loop(0, chunks, project, 0)

    def s_copy(i):
        return remote(stats.at[0], stats.at[i], ss.at[i], sr.at[i], dev(lax.rem(chip + i, nc)))

    def k_copy(i):
        return remote(sums.at[0], sums.at[i], ks.at[i], kr.at[i], dev(lax.rem(chip + i, nc)))

    for i in range(1, nc):
        k_copy(i).start()
    means, squares = [], []
    for i in range(n_mp // per):
        b, at = spot(i)
        value = fdot(pieces(i), xt[...]).astype(BF16)
        e[b, at:at + lump, :] = value
        value = value.astype(F32)
        mean = jnp.mean(value, axis=0, keepdims=True)
        center = value - mean
        means.append(mean)
        squares.append(jnp.sum(center * center, axis=0, keepdims=True))
    mean = sum(means) * (1.0 / len(means))
    square = sum(squares)
    for one in means:
        square = square + lump * ((one - mean) * (one - mean))
    stats[0, 0:1, :] = mean
    stats[0, 1:2, :] = square
    for i in range(1, nc):
        s_copy(i).start()

    def fold(k, carry):
        for u in range(1, side):
            a_copy(k, u).wait_recv()
        for v in range(1, side):
            value = pf[k, chip_at(way(k), 0, v)]
            for u in range(1, side):
                value = value + r1[k, u, v].astype(F32)
            s2b[k, v] = value.astype(BF16)
            b_copy(k, v).start()
        value = pf[k, chip]
        for u in range(1, side):
            value = value + r1[k, u, 0].astype(F32)
        raw[k] = value
        return carry

    lax.fori_loop(0, chunks - 1, fold, 0)

    for i in range(1, nc):
        s_copy(i).wait_recv()
    mean = sum(stats[i, 0:1, :] for i in range(nc)) * (1.0 / nc)
    square = jnp.zeros((1, group), F32)
    for i in range(nc):
        gap = stats[i, 0:1, :] - mean
        square = square + stats[i, 1:2, :] + (2.0 * block) * (gap * gap)
    scale = lax.rsqrt(square * (1.0 / (2.0 * block * nc)) + 1e-06)
    line = lax.broadcasted_iota(jnp.int32, (128, group), 0)
    both = jnp.where(line == 0, scale, 0.0)
    for i in range(nc):
        both = jnp.where(line == 1 + i, stats[i, 0:1, :] - mean, both)
    of_row[...] = both.T
    step = 384 if block % 384 == 0 else block
    for b in range(2):
        for at in range(0, block, step):
            value = (e[b, at:at + step, :].astype(F32) - mean) * scale
            e[b, at:at + step, :] = value.astype(BF16)
    n_copy = remote(e.at[1 - core], nto, ns, nr, {"dp": partner})
    n_copy.start()
    fold(chunks - 1, 0)
    for i in range(1, nc):
        k_copy(i).wait_recv()

    root = 1.0 / math.sqrt(HD)
    per_total = 1.0 / total_f

    def g_first(k, u):
        return remote(gath.at[k, 0, chip], gath.at[k, 0, chip], gs.at[k, u], gr.at[k, u], dev(chip_at(way(k), u, 0)))

    def g_second(k, u, v):
        at = chip_at(way(k), -u, 0)
        return remote(gath.at[k, 0, at], gath.at[k, 0, at], hs.at[k, u, v], hr.at[k, u, v], dev(chip_at(way(k), 0, v)))

    def g_across(k, u, v):
        at = chip_at(way(k), -u, -v)
        return remote(gath.at[k, 0, at], gath.at[k, 1, at], cs.at[k, u, v], cr.at[k, u, v], {"dp": partner})

    def attend(k):
        for v in range(1, side):
            b_copy(k, v).wait_recv()
        mask, alive = allow[...], live[...]
        mine_rows = of_row[pl.ds(pl.multiple_of(chip * keep, keep), keep), :]
        row_scale = mine_rows[:, 0:1]
        gaps = [jnp.broadcast_to(mine_rows[:, 1 + i:2 + i], (keep, HD)) for i in range(nc)]
        error_sum = jnp.zeros((8, HD), F32)
        for h in range(hp):
            part_of = []
            for s in range(3):
                cols = slice(s * wide + h * HD, s * wide + (h + 1) * HD)
                value = raw[k, :, cols]
                for v in range(1, side):
                    value = value + r2[k, v, :, cols].astype(F32)
                for i in range(nc):
                    value = value + gaps[i] * sums[i, k, s * hp + h:s * hp + h + 1, :]
                part_of.append(value * row_scale)
            q_unit, q_scale = layer_parts(part_of[0])
            k_unit, k_scale = layer_parts(part_of[1])
            q_n, k_n, v_n = q_unit.astype(BF16), k_unit.astype(BF16), part_of[2].astype(BF16)
            scores = fdot(q_n, k_n, ((1,), (1,))) * root
            power = jnp.where(mask > 0.0, jnp.exp(scores), 0.0)
            below = jnp.sum(power, axis=-1, keepdims=True)
            below = jnp.where(below > 0.0, below, 1.0)
            weights = (power / below).astype(BF16)
            want = tgt[:, pl.ds(pl.multiple_of(k * wide + h * HD, HD), HD)]
            error = jnp.where(alive > 0.0, fdot(weights, v_n) - want, 0.0)
            error_sum = error_sum + jnp.sum((error * error).reshape(keep // 8, 8, HD), axis=0)
            out_grad = (error * per_total).astype(BF16)
            prob_grad = fdot(out_grad, v_n, ((1,), (1,)))
            value_grad = fdot(weights, out_grad, ((0,), (0,)))
            weight_f = weights.astype(F32)
            score_grad = (
                weight_f * (prob_grad - jnp.sum(prob_grad * weight_f, axis=-1, keepdims=True)) * root
            ).astype(BF16)
            q_grad = norm_grad(q_unit, q_scale, fdot(score_grad, k_n))
            k_grad = norm_grad(k_unit, k_scale, fdot(score_grad, q_n, ((0,), (0,))))
            for s, value in enumerate((q_grad, k_grad, value_grad)):
                gath[k, 0, chip, :, s * wide + h * HD:s * wide + (h + 1) * HD] = value.astype(BF16)
        sq[...] += error_sum
        for u in range(1, side):
            g_first(k, u).start()
        for v in range(1, side):
            g_second(k, 0, v).start()
        g_across(k, 0, 0).start()

    def relay(k):
        for u in range(1, side):
            g_first(k, u).wait_recv()
            for v in range(1, side):
                g_second(k, u, v).start()
            g_across(k, u, 0).start()

    def cross(k):
        for u in range(side):
            for v in range(1, side):
                g_second(k, u, v).wait_recv()
                g_across(k, u, v).start()

    def o_copy(k):
        cols = pl.ds(pl.multiple_of(k * wide, wide), wide)
        return pltpu.make_async_copy(stage.at[k], out.at[:, :, cols], os.at[k])

    def finish(k):
        for u in range(side):
            for v in range(side):
                g_across(k, u, v).wait_recv()
        right = gath[k].reshape(2 * group, 3 * wide)
        left = jnp.concatenate([e[core], nto[...]], axis=1)
        value = fdot(left, right)
        for s in range(3):
            stage[k, s] = value[:, s * wide:(s + 1) * wide]
        o_copy(k).start()

    n_copy.wait_recv()

    def y_copy(i):
        return remote(sq, zsq.at[i], zs.at[i], zr.at[i], {"mp": lax.rem(m + i, n_mp)})

    def l_copy(i):
        return remote(mine, psq.at[i], qs.at[i], qr.at[i], {"dp": lax.rem(d + i, n)})

    def flow(i, carry):
        @pl.when(i < chunks)
        def _():
            attend(i)

        @pl.when(i == chunks - 1)
        def _():
            for j in range(1, n_mp):
                y_copy(j).start()

        @pl.when((i >= 1) & (i <= chunks))
        def _():
            relay(i - 1)

        @pl.when(i == chunks)
        def _():
            value = sq[...]
            for j in range(1, n_mp):
                y_copy(j).wait_recv()
                value = value + zsq[j]
            mine[...] = value
            for j in range(1, n):
                l_copy(j).start()

        @pl.when((i >= 2) & (i <= chunks + 1))
        def _():
            cross(i - 2)

        @pl.when(i >= 3)
        def _():
            finish(i - 3)

        return carry

    lax.fori_loop(0, chunks + 2, flow, 0)

    finish(chunks - 1)
    value = mine[...]
    for i in range(1, n):
        l_copy(i).wait_recv()
        value = value + psq[i]
    value = jnp.sum(jnp.sum(value, axis=1, keepdims=True), axis=0, keepdims=True)
    loss[...] = jnp.broadcast_to(value * (0.5 * per_total), loss.shape)

    for u in range(1, side):
        p_first(u).wait_send()
    for v in range(1, side):
        for u in range(side):
            p_second(u, v).wait_send()
    for i in range(1, n):
        m_copy(i).wait_send()
        l_copy(i).wait_send()
    for i in range(1, n_mp):
        y_copy(i).wait_send()
    for c in range(zc):
        for i in range(n_mp - 1):
            for up in (True, False):
                @pl.when(z_sends(up, i))
                def _():
                    z_copy(up, i, c).wait_send()
        for i in range(n_mp):
            f_copy(i, c).wait_send()

            @pl.when(owner(i) != chip)
            def _():
                e_copy(i, zbuf.at[i, c], c).wait_send()

    @pl.when(is_low == 0)
    def _():
        t_copy().wait_send()

    w_swap.wait_send()
    n_copy.wait_send()
    for i in range(1, nc):
        s_copy(i).wait_send()
        k_copy(i).wait_send()

    def drain(k, carry):
        for u in range(1, side):
            a_copy(k, u).wait_send()
            g_first(k, u).wait_send()
        for v in range(1, side):
            b_copy(k, v).wait_send()
            for u in range(side):
                g_second(k, u, v).wait_send()
        for u in range(side):
            for v in range(side):
                g_across(k, u, v).wait_send()
        o_copy(k).wait()
        return carry

    lax.fori_loop(0, chunks, drain, 0)


def run_block(patches, embed, weight, counts, targets, n, n_mp):
    length, rows = patches.shape
    piece = embed.shape[0]
    columns = weight.shape[2]
    heads = columns // HD
    nc = n // 2
    side = grid_side(nc)
    keep = rows * 3 // 4
    group = nc * keep
    block = n_mp * piece
    imgs = counts.shape[0]
    assert n % (2 * n_mp) == 0 and block == weight.shape[1]
    zc = 4 if piece % 64 == 0 else 1
    hp = 2 if heads % 2 == 0 else 1
    chunks = heads // hp
    wide = 3 * hp * HD
    dma = lambda *k: pltpu.SemaphoreType.DMA(k) if k else pltpu.SemaphoreType.DMA
    anywhere = pl.BlockSpec(memory_space=pl.ANY)
    vmem = pl.BlockSpec(memory_space=pltpu.VMEM)
    v = pltpu.VMEM
    return pl.pallas_call(
        functools.partial(block_kernel, n, n_mp, zc, hp),
        out_shape=(
            jax.ShapeDtypeStruct((3, block, columns), F32),
            jax.ShapeDtypeStruct((8, 128), F32),
        ),
        in_specs=[anywhere, anywhere, anywhere, pl.BlockSpec(memory_space=pltpu.SMEM), anywhere],
        out_specs=(anywhere, vmem),
        scratch_shapes=[
            v((nc, length, rows), BF16),
            v((n_mp, zc, piece // zc, length), BF16),
            v((2 * n_mp, zc, piece // zc, length), BF16),
            v((2,) + weight.shape, BF16),
            v((length, group), BF16),
            v((group, length), BF16),
            v((2, block, group), BF16),
            v((block, group), BF16),
            v((2, group + 16, block), BF16),
            v((group, 128), F32),
            v((group, 128), F32),
            v((nc, chunks, 8, HD), F32),
            v((nc, 8, group), F32),
            v((n, imgs, 128), jnp.int32),
            v((rows, columns), BF16),
            v((keep, columns), BF16),
            v((keep, columns), F32),
            v((keep, keep), F32),
            v((keep, HD), F32),
            v((chunks, nc, keep, wide), F32),
            v((chunks, side, side, keep, wide), BF16),
            v((chunks, side, side, keep, wide), BF16),
            v((chunks, side, keep, wide), BF16),
            v((chunks, keep, wide), F32),
            v((chunks, side, keep, wide), BF16),
            v((chunks, 2, nc, keep, wide), BF16),
            v((chunks, 3, block, hp * HD), F32),
            v((8, 128), F32),
            v((n_mp, 8, 128), F32),
            v((n, 8, 128), F32),
            v((8, 128), F32),
            dma(), dma(), dma(),
            dma(n), dma(n),
            dma(side, side), dma(side, side),
            dma(n_mp, zc), dma(n_mp, zc), dma(n_mp, zc), dma(n_mp, zc),
            dma(n_mp, zc), dma(n_mp, zc), dma(zc),
            dma(n_mp, zc), dma(n_mp, zc),
            dma(), dma(), dma(),
            dma(nc), dma(nc), dma(nc), dma(nc),
            dma(), dma(),
            dma(chunks, side), dma(chunks, side),
            dma(chunks, side), dma(chunks, side),
            dma(chunks, side), dma(chunks, side),
            dma(chunks, side, side), dma(chunks, side, side),
            dma(chunks, side, side), dma(chunks, side, side),
            dma(n_mp), dma(n_mp), dma(n), dma(n),
            dma(chunks),
        ],
        compiler_params=pltpu.CompilerParams(
            collective_id=0, has_side_effects=True, vmem_limit_bytes=VMEM_BYTES
        ),
    )(patches, embed, weight, counts, targets)


def local(n, n_mp, patches, embed_weight, project_weight, patch_counts, segment_ids, targets):
    del segment_ids
    weight_grad, loss = run_block(
        patches.T, embed_weight, jnp.transpose(project_weight, (1, 0, 2)), patch_counts, targets, n, n_mp
    )
    return (jnp.transpose(weight_grad, (1, 0, 2)), loss[0, 0])


def solution(mesh):
    in_specs = (
        P("dp", None),
        P(("mp", "dp"), None),
        P("dp", None, "mp"),
        P("dp"),
        P("dp"),
        P("dp", "mp"),
    )
    out_specs = (P("dp", None, "mp"), P())
    return jax.shard_map(
        functools.partial(local, mesh.shape["dp"], mesh.shape["mp"]), mesh=mesh, in_specs=in_specs, out_specs=out_specs, check_vma=False)
```

```python
import functools
import math

import jax
import jax.numpy as jnp
from jax import lax
from jax.experimental import pallas as pl
from jax.experimental.pallas import tpu as pltpu
from jax.sharding import PartitionSpec as P

HD = 128
MESH = pl.DeviceIdType.MESH
VMEM_BYTES = 62 * 1024 * 1024
F32, BF16 = jnp.float32, jnp.bfloat16


def remote(src, dst, send_sem, recv_sem, device_id):
    return pltpu.make_async_remote_copy(
        src_ref=src, dst_ref=dst, send_sem=send_sem, recv_sem=recv_sem,
        device_id=device_id, device_id_type=MESH,
    )


def greet(n, n_mp, d, m):
    barrier = pltpu.get_barrier_semaphore()
    for i in range(1, n):
        pl.semaphore_signal(barrier, inc=1, device_id={"dp": lax.rem(d + i, n)}, device_id_type=MESH)
    for i in range(1, n_mp):
        pl.semaphore_signal(barrier, inc=1, device_id={"mp": lax.rem(m + i, n_mp)}, device_id_type=MESH)
    pl.semaphore_wait(barrier, n - 1 + n_mp - 1)


def grid_side(nc):
    side = math.isqrt(nc)
    assert side * side == nc
    return side


def fdot(a, b, dims=((1,), (0,))):
    return lax.dot_general(a, b, (dims, ((), ())), preferred_element_type=F32)


def layer_parts(x):
    center = x - jnp.mean(x, axis=-1, keepdims=True)
    scale = lax.rsqrt(jnp.mean(center * center, axis=-1, keepdims=True) + 1e-06)
    return center * scale, scale


def norm_grad(unit, scale, g):
    along = jnp.mean(g * unit, axis=-1, keepdims=True)
    return scale * (g - jnp.mean(g, axis=-1, keepdims=True) - unit * along)


def block_kernel(
    n, n_mp, zc, hp,
    patches, embed, weight, counts, targets,
    left, grads, loss,
    pall, zbuf, wp, wbuf, xt, xn, e, nto, nrm, center_of, of_row, sums, stats, metas, town, ttail, tgt,
    allow, live, pf, sb, r1, s2b, raw, r2, gath, sq, zsq, psq, mine,
    w_sem, wx, wy, ms, mr, ps, pr, us, ur, vs, vr, es, er, el, fs, fr, ts, tr, tl,
    ss, sr, ks, kr, ns, nr, as_, ar, bs, br, gs, gr, hs, hr, cs, cr, zs, zr, qs, qr, os, ls,
):
    d, m = lax.axis_index("dp"), lax.axis_index("mp")
    core, chip = lax.rem(d, 2), d // 2
    partner = d + 1 - 2 * core
    nc = n // 2
    side = grid_side(nc)
    cx, cy = lax.rem(chip, side), chip // side
    rows = targets.shape[0]
    keep = rows * 3 // 4
    low = rows - keep
    group = nc * keep
    piece = embed.shape[0]
    part = piece // zc
    block = n_mp * piece
    span = n // (2 * n_mp)
    imgs = counts.shape[0]
    chunks = pf.shape[0]
    wide = hp * HD
    pair = lax.rem(d + n // 2, n)
    is_low = jnp.where(d < n // 2, 1, 0)

    def chip_at(h, u, v):
        dx = u * (1 - h) + v * h
        dy = u * h + v * (1 - h)
        return lax.rem(cy + dy + side, side) * side + lax.rem(cx + dx + side, side)

    def dev(c):
        return {"dp": 2 * c + core}

    w_own = pltpu.make_async_copy(weight, wbuf.at[core], w_sem)
    w_own.start()
    t_own = pltpu.make_async_copy(targets, town, tl)
    t_own.start()
    p_local = pltpu.make_async_copy(patches, pall.at[chip], ps.at[0, 0])
    p_local.start()
    cum = jnp.zeros((imgs, 128), jnp.int32)
    line = lax.broadcasted_iota(jnp.int32, (imgs, 128), 0)
    total = jnp.int32(0)
    for s in range(imgs):
        total = total + counts[s]
        cum = jnp.where(line == s, total, cum)
    metas[d] = cum

    greet(n, n_mp, d, m)

    def p_first(u):
        return remote(patches, pall.at[chip], ps.at[u, 0], pr.at[u, 0], dev(chip_at(core, u, 0)))

    def p_second(u, v):
        at = chip_at(core, -u, 0)
        src = patches if u == 0 else pall.at[at]
        return remote(src, pall.at[at], ps.at[u, v], pr.at[u, v], dev(chip_at(core, 0, v)))

    def m_copy(i):
        return remote(metas.at[d], metas.at[d], ms.at[i], mr.at[i], {"dp": lax.rem(d + i, n)})

    for u in range(1, side):
        p_first(u).start()
    for v in range(1, side):
        p_second(0, v).start()

    def z_copy(up, i, c):
        origin = m - i if up else m + i
        src = embed.at[pl.ds(c * part, part)] if i == 0 else zbuf.at[origin, c]
        send, recv = (us, ur) if up else (vs, vr)
        return remote(src, zbuf.at[origin, c], send.at[i, c], recv.at[i + 1, c], {"mp": m + 1 if up else m - 1})

    def z_wait(up, i, c):
        origin = m - i if up else m + i
        send, recv = (us, ur) if up else (vs, vr)
        remote(zbuf.at[origin, c], zbuf.at[origin, c], send.at[i, c], recv.at[i, c], {"mp": m - 1 if up else m + 1}).wait_recv()

    def z_has(up, i):
        return m - i >= 0 if up else m + i <= n_mp - 1

    def z_sends(up, i):
        return (m - i >= 0) & (m < n_mp - 1) if up else (m + i <= n_mp - 1) & (m > 0)

    slot = lax.rem(d, 2 * n_mp)
    rel_own = lax.rem(chip, n_mp)

    def owner(origin):
        return origin * span + d // (2 * n_mp)

    def e_copy(origin, src, c):
        return remote(src, wp.at[slot, c], es.at[origin, c], er.at[rel_own, c], dev(owner(origin)))

    def e_local(src, c):
        return pltpu.make_async_copy(src, wp.at[slot, c], el.at[c])

    def e_start(origin, own, c):
        src = embed.at[pl.ds(c * part, part)] if own else zbuf.at[origin, c]

        @pl.when(owner(origin) != chip)
        def _():
            e_copy(origin, src, c).start()

        @pl.when(owner(origin) == chip)
        def _():
            e_local(src, c).start()

    def z_own(c):
        for up in (True, False):
            @pl.when(z_sends(up, 0))
            def _():
                z_copy(up, 0, c).start()
        e_start(m, True, c)

    for c in range(min(2, zc)):
        z_own(c)
    for i in range(1, n):
        m_copy(i).start()

    w_swap = remote(weight, wbuf.at[core], wx, wy, {"dp": partner})
    w_swap.start()

    p_local.wait()
    for u in range(1, side):
        p_first(u).wait_recv()
        for v in range(1, side):
            p_second(u, v).start()

    def t_copy():
        return remote(town.at[pl.ds(low, keep)], ttail, ts, tr, {"dp": pair})

    t_own.wait()

    @pl.when(is_low == 1)
    def _():
        sq[...] = jnp.zeros_like(sq)

    @pl.when(is_low == 0)
    def _():
        sq[...] = jnp.zeros_like(sq)
        ttail[...] = jnp.zeros_like(ttail)

    def z_wave(w):
        for i in range(1, n_mp):
            c = w + 1 - i
            if 0 <= c < zc:
                for up in (True, False):
                    @pl.when(z_has(up, i))
                    def _():
                        z_wait(up, i, c)
                        if i < n_mp - 1:
                            @pl.when(z_sends(up, i))
                            def _():
                                z_copy(up, i, c).start()
                        e_start(m - i if up else m + i, False, c)
        if w + 2 < zc:
            z_own(w + 2)

    waves = zc + n_mp - 2
    for w in range(waves // 2):
        z_wave(w)

    for v in range(1, side):
        for u in range(side):
            p_second(u, v).wait_recv()
    for i in range(1, n):
        m_copy(i).wait_recv()

    def ends(meta):
        fits = jnp.zeros((1, 1), jnp.int32)
        for s in range(imgs):
            at = meta[s:s + 1, 0:1]
            fits = jnp.maximum(fits, jnp.where(at <= keep, at, 0))
        return fits, meta[imgs - 1:imgs, 0:1]

    lane = lax.broadcasted_iota(jnp.int32, (1, group), 1)
    source = jnp.full((1, group), -1, jnp.int32)
    for j in range(nc // 2):
        far = j + nc // 2
        _, held = ends(metas[2 * j + core])
        fits, full = ends(metas[2 * far + core])
        r = lane - j * keep
        tail = fits + r - held
        at = jnp.where(r < held, j * rows + r, jnp.where(tail < full, far * rows + tail, -1))
        source = jnp.where((r >= 0) & (r < keep), at, source)
        r = lane - far * keep
        source = jnp.where((r >= 0) & (r < fits) & (r < keep), far * rows + r, source)
    picked = None
    for j in range(nc):
        place_of = lax.broadcasted_iota(jnp.int32, (rows, group), 0) + j * rows
        pick = jnp.where(place_of == source, 1.0, 0.0).astype(BF16)
        term = fdot(pall[j], pick)
        picked = term if picked is None else picked + term
    xt[...] = picked.astype(BF16)
    xn[...] = picked.astype(BF16).T
    for b in range(2):
        nrm[b, group:group + 16, :] = jnp.ones((16, block), BF16)

    fits_own, full_own = ends(metas[d])
    fits_far, full_far = ends(metas[pair])
    limit = is_low * full_own + (1 - is_low) * fits_own

    def place(shape, dim):
        r = lax.broadcasted_iota(jnp.int32, shape, dim)
        tail = fits_far + r - limit
        near = r < limit
        moved = (r >= limit) & (tail < full_far) & (is_low == 1)
        return r, tail, near, moved

    def ident(shape, dim):
        r, tail, near, moved = place(shape, dim)
        first = jnp.zeros(shape, jnp.int32)
        second = jnp.full(shape, imgs, jnp.int32)
        mine_, theirs = metas[d], metas[pair]
        for s in range(imgs):
            first = first + jnp.where(mine_[s:s + 1, 0:1] <= r, 1, 0)
            second = second + jnp.where(theirs[s:s + 1, 0:1] <= tail, 1, 0)
        return jnp.where(near, first, jnp.where(moved, second, -1))

    down, over = ident((keep, keep), 0), ident((keep, keep), 1)
    allow[...] = jnp.where((down == over) & (down >= 0), 1.0, 0.0)
    live[...] = jnp.where(ident((keep, HD), 0) >= 0, 1.0, 0.0)
    total_f = jnp.zeros((1, 1), jnp.int32)
    for i in range(n):
        total_f = total_f + metas[i][imgs - 1:imgs, 0:1]
    total_f = total_f.astype(F32)

    for w in range(waves // 2, waves):
        z_wave(w)

    base = n_mp * lax.rem(chip, span)

    def f_copy(i, c):
        q = 2 * i + core
        return remote(wp.at[q, c], wp.at[q, c], fs.at[i, c], fr.at[i, c], {"dp": partner})

    for c in range(zc):
        for i in range(n_mp):
            @pl.when(base + i == chip)
            def _():
                e_local(zbuf.at[0, c], c).wait()

            @pl.when(base + i != chip)
            def _():
                q = 2 * i + core
                remote(wp.at[q, c], wp.at[q, c], es.at[i, c], er.at[i, c], {"dp": partner}).wait_recv()

            f_copy(i, c).start()

    @pl.when(is_low == 0)
    def _():
        t_copy().start()

    per = 1 if 2 * piece % 128 == 0 else n_mp // 2
    lump = 2 * piece * per

    def pieces(i):
        return jnp.concatenate(
            [wp[2 * j + k, c] for j in range(i * per, (i + 1) * per) for k in range(2) for c in range(zc)], axis=0
        )

    def spot(i):
        return divmod(i * lump, block)

    for i in range(n_mp // per):
        for j in range(i * per, (i + 1) * per):
            for c in range(zc):
                f_copy(j, c).wait_recv()
        b, at = spot(i)
        nrm[b, 0:group, at:at + lump] = fdot(xn[...], pieces(i), ((1,), (1,))).astype(BF16)
    ones = jnp.ones((block, 128), BF16)
    about = (fdot(nrm[0, 0:group, :], ones) + fdot(nrm[1, 0:group, :], ones)) * (0.5 / block)
    center_of[...] = about
    w_own.wait()
    w_swap.wait_recv()

    def way(k):
        return lax.rem(k + core, 2)

    def a_copy(k, u):
        return remote(sb.at[k, u], r1.at[k, u], as_.at[k, u], ar.at[k, u], dev(chip_at(way(k), u, 0)))

    def b_copy(k, v):
        return remote(s2b.at[k, v], r2.at[k, v], bs.at[k, v], br.at[k, v], dev(chip_at(way(k), 0, v)))

    ahead = chunks - 1 if chunks > 2 else chunks

    def project(k, carry):
        acc = None
        for b in range(2):
            cols = jnp.concatenate(
                [wbuf[b, s, :, pl.ds(pl.multiple_of(k * wide, wide), wide)] for s in range(3)], axis=1
            )
            term = fdot(nrm[b], cols)
            acc = term if acc is None else acc + term
        for s in range(3 * hp):
            sums[0, k, s:s + 1, :] = acc[group:group + 1, s * HD:(s + 1) * HD]
        center = jnp.concatenate([center_of[...]] * (3 * hp), axis=1)
        pf[k] = (acc[0:group] - center * acc[group:group + 1]).reshape(nc, keep, 3 * wide)
        for u in range(1, side):
            for v in range(side):
                sb[k, u, v] = pf[k, chip_at(way(k), u, v)].astype(BF16)

            @pl.when(k < ahead)
            def _():
                a_copy(k, u).start()
        return carry

    lax.fori_loop(0, chunks, project, 0)

    def s_copy(i):
        return remote(stats.at[0], stats.at[i], ss.at[i], sr.at[i], dev(lax.rem(chip + i, nc)))

    def k_copy(i):
        return remote(sums.at[0], sums.at[i], ks.at[i], kr.at[i], dev(lax.rem(chip + i, nc)))

    for i in range(1, nc):
        k_copy(i).start()
    means, squares = [], []
    for i in range(n_mp // per):
        b, at = spot(i)
        value = fdot(pieces(i), xt[...]).astype(BF16)
        e[b, at:at + lump, :] = value
        value = value.astype(F32)
        mean = jnp.mean(value, axis=0, keepdims=True)
        center = value - mean
        means.append(mean)
        squares.append(jnp.sum(center * center, axis=0, keepdims=True))
    mean = sum(means) * (1.0 / len(means))
    square = sum(squares)
    for one in means:
        square = square + lump * ((one - mean) * (one - mean))
    stats[0, 0:1, :] = mean
    stats[0, 1:2, :] = square
    for i in range(1, nc):
        s_copy(i).start()

    @pl.when(is_low == 1)
    def _():
        t_copy().wait_recv()

    r, tail, near, moved = place((keep, rows), 0)
    col = lax.broadcasted_iota(jnp.int32, (keep, rows), 1)
    pick_own = jnp.where(near & (col == r), 1.0, 0.0).astype(BF16)
    r, tail, near, moved = place((keep, keep), 0)
    col = lax.broadcasted_iota(jnp.int32, (keep, keep), 1)
    pick_far = jnp.where(moved & (col == tail - low), 1.0, 0.0).astype(BF16)
    tgt[...] = fdot(pick_own, town[...]) + fdot(pick_far, ttail[...])

    def fold(k, carry):
        for u in range(1, side):
            a_copy(k, u).wait_recv()
        for v in range(1, side):
            value = pf[k, chip_at(way(k), 0, v)]
            for u in range(1, side):
                value = value + r1[k, u, v].astype(F32)
            s2b[k, v] = value.astype(BF16)
            b_copy(k, v).start()
        value = pf[k, chip]
        for u in range(1, side):
            value = value + r1[k, u, 0].astype(F32)
        raw[k] = value
        return carry

    fold(0, 0)
    for k in range(ahead, chunks):
        for u in range(1, side):
            a_copy(k, u).start()
    if ahead > 1:
        lax.fori_loop(1, ahead, fold, 0)

    for i in range(1, nc):
        s_copy(i).wait_recv()
    mean = sum(stats[i, 0:1, :] for i in range(nc)) * (1.0 / nc)
    square = jnp.zeros((1, group), F32)
    for i in range(nc):
        gap = stats[i, 0:1, :] - mean
        square = square + stats[i, 1:2, :] + (2.0 * block) * (gap * gap)
    scale = lax.rsqrt(square * (1.0 / (2.0 * block * nc)) + 1e-06)
    line = lax.broadcasted_iota(jnp.int32, (128, group), 0)
    both = jnp.where(line == 0, scale, 0.0)
    for i in range(nc):
        both = jnp.where(line == 1 + i, stats[i, 0:1, :] - mean, both)
    of_row[...] = both.T
    step = 384 if block % 384 == 0 else block
    for b in range(2):
        for at in range(0, block, step):
            value = (e[b, at:at + step, :].astype(F32) - mean) * scale
            e[b, at:at + step, :] = value.astype(BF16)
    n_copy = remote(e.at[1 - core], nto, ns, nr, {"dp": partner})
    n_copy.start()
    for i in range(1, nc):
        k_copy(i).wait_recv()

    root = 1.0 / math.sqrt(HD)
    per_total = 1.0 / total_f

    def g_first(k, u):
        return remote(gath.at[k, 0, chip], gath.at[k, 0, chip], gs.at[k, u], gr.at[k, u], dev(chip_at(way(k), u, 0)))

    def g_second(k, u, v):
        at = chip_at(way(k), -u, 0)
        return remote(gath.at[k, 0, at], gath.at[k, 0, at], hs.at[k, u, v], hr.at[k, u, v], dev(chip_at(way(k), 0, v)))

    def g_across(k, u, v):
        at = chip_at(way(k), -u, -v)
        return remote(gath.at[k, 0, at], gath.at[k, 1, at], cs.at[k, u, v], cr.at[k, u, v], {"dp": partner})

    def attend(k):
        for v in range(1, side):
            b_copy(k, v).wait_recv()
        mask, alive = allow[...], live[...]
        mine_rows = of_row[pl.ds(pl.multiple_of(chip * keep, keep), keep), :]
        row_scale = mine_rows[:, 0:1]
        gaps = [jnp.broadcast_to(mine_rows[:, 1 + i:2 + i], (keep, HD)) for i in range(nc)]
        error_sum = jnp.zeros((8, HD), F32)
        for h in range(hp):
            part_of = []
            for s in range(3):
                cols = slice(s * wide + h * HD, s * wide + (h + 1) * HD)
                value = raw[k, :, cols]
                for v in range(1, side):
                    value = value + r2[k, v, :, cols].astype(F32)
                for i in range(nc):
                    value = value + gaps[i] * sums[i, k, s * hp + h:s * hp + h + 1, :]
                part_of.append(value * row_scale)
            q_unit, q_scale = layer_parts(part_of[0])
            k_unit, k_scale = layer_parts(part_of[1])
            q_n, k_n, v_n = q_unit.astype(BF16), k_unit.astype(BF16), part_of[2].astype(BF16)
            scores = fdot(q_n, k_n, ((1,), (1,))) * root
            power = jnp.where(mask > 0.0, jnp.exp(scores), 0.0)
            below = jnp.sum(power, axis=-1, keepdims=True)
            below = jnp.where(below > 0.0, below, 1.0)
            weights = (power / below).astype(BF16)
            want = tgt[:, pl.ds(pl.multiple_of(k * wide + h * HD, HD), HD)]
            error = jnp.where(alive > 0.0, fdot(weights, v_n) - want, 0.0)
            error_sum = error_sum + jnp.sum((error * error).reshape(keep // 8, 8, HD), axis=0)
            out_grad = (error * per_total).astype(BF16)
            prob_grad = fdot(out_grad, v_n, ((1,), (1,)))
            value_grad = fdot(weights, out_grad, ((0,), (0,)))
            weight_f = weights.astype(F32)
            score_grad = (
                weight_f * (prob_grad - jnp.sum(prob_grad * weight_f, axis=-1, keepdims=True)) * root
            ).astype(BF16)
            q_grad = norm_grad(q_unit, q_scale, fdot(score_grad, k_n))
            k_grad = norm_grad(k_unit, k_scale, fdot(score_grad, q_n, ((0,), (0,))))
            for s, value in enumerate((q_grad, k_grad, value_grad)):
                gath[k, 0, chip, :, s * wide + h * HD:s * wide + (h + 1) * HD] = value.astype(BF16)
        sq[...] += error_sum
        for u in range(1, side):
            g_first(k, u).start()
        for v in range(1, side):
            g_second(k, 0, v).start()
        g_across(k, 0, 0).start()

    def relay(k):
        for u in range(1, side):
            g_first(k, u).wait_recv()
            for v in range(1, side):
                g_second(k, u, v).start()
            g_across(k, u, 0).start()

    def cross(k):
        for u in range(side):
            for v in range(1, side):
                g_second(k, u, v).wait_recv()
                g_across(k, u, v).start()

    def o_copy(k):
        return pltpu.make_async_copy(gath.at[k], grads.at[k], os.at[k])

    def finish(k):
        for u in range(side):
            for v in range(side):
                g_across(k, u, v).wait_recv()
        o_copy(k).start()

    def left_copy(i):
        return pltpu.make_async_copy(nto if i else e.at[core], left.at[i], ls.at[i])

    left_copy(0).start()
    n_copy.wait_recv()
    left_copy(1).start()

    def y_copy(i):
        return remote(sq, zsq.at[i], zs.at[i], zr.at[i], {"mp": lax.rem(m + i, n_mp)})

    def l_copy(i):
        return remote(mine, psq.at[i], qs.at[i], qr.at[i], {"dp": lax.rem(d + i, n)})

    def flow(i, carry):
        @pl.when(i < chunks)
        def _():
            attend(i)

        @pl.when((i >= 0) & (i < chunks - ahead))
        def _():
            fold(ahead + i, 0)

        @pl.when(i == chunks - 1)
        def _():
            for j in range(1, n_mp):
                y_copy(j).start()

        @pl.when((i >= 1) & (i <= chunks))
        def _():
            relay(i - 1)

        @pl.when(i == chunks)
        def _():
            value = sq[...]
            for j in range(1, n_mp):
                y_copy(j).wait_recv()
                value = value + zsq[j]
            mine[...] = value
            for j in range(1, n):
                l_copy(j).start()

        @pl.when((i >= 2) & (i <= chunks + 1))
        def _():
            cross(i - 2)

        @pl.when(i >= 3)
        def _():
            finish(i - 3)

        return carry

    lax.fori_loop(0, chunks + 2, flow, 0)

    finish(chunks - 1)
    value = mine[...]
    for i in range(1, n):
        l_copy(i).wait_recv()
        value = value + psq[i]
    value = jnp.sum(jnp.sum(value, axis=1, keepdims=True), axis=0, keepdims=True)
    loss[...] = jnp.broadcast_to(value * (0.5 * per_total), loss.shape)

    for u in range(1, side):
        p_first(u).wait_send()
    for v in range(1, side):
        for u in range(side):
            p_second(u, v).wait_send()
    for i in range(1, n):
        m_copy(i).wait_send()
        l_copy(i).wait_send()
    for i in range(1, n_mp):
        y_copy(i).wait_send()
    for c in range(zc):
        for i in range(n_mp - 1):
            for up in (True, False):
                @pl.when(z_sends(up, i))
                def _():
                    z_copy(up, i, c).wait_send()
        for i in range(n_mp):
            f_copy(i, c).wait_send()

            @pl.when(owner(i) != chip)
            def _():
                e_copy(i, zbuf.at[i, c], c).wait_send()

    @pl.when(is_low == 0)
    def _():
        t_copy().wait_send()

    w_swap.wait_send()
    n_copy.wait_send()
    for i in range(2):
        left_copy(i).wait()
    for i in range(1, nc):
        s_copy(i).wait_send()
        k_copy(i).wait_send()

    def drain(k, carry):
        for u in range(1, side):
            a_copy(k, u).wait_send()
            g_first(k, u).wait_send()
        for v in range(1, side):
            b_copy(k, v).wait_send()
            for u in range(side):
                g_second(k, u, v).wait_send()
        for u in range(side):
            for v in range(side):
                g_across(k, u, v).wait_send()
        o_copy(k).wait()
        return carry

    lax.fori_loop(0, chunks, drain, 0)


def run_block(patches, embed, weight, counts, targets, n, n_mp):
    length, rows = patches.shape
    piece = embed.shape[0]
    columns = weight.shape[2]
    heads = columns // HD
    nc = n // 2
    side = grid_side(nc)
    keep = rows * 3 // 4
    group = nc * keep
    block = n_mp * piece
    imgs = counts.shape[0]
    assert n % (2 * n_mp) == 0 and block == weight.shape[1]
    zc = 4 if piece % 64 == 0 else 1
    hp = 2 if heads % 2 == 0 else 1
    chunks = heads // hp
    wide = 3 * hp * HD
    dma = lambda *k: pltpu.SemaphoreType.DMA(k) if k else pltpu.SemaphoreType.DMA
    anywhere = pl.BlockSpec(memory_space=pl.ANY)
    vmem = pl.BlockSpec(memory_space=pltpu.VMEM)
    v = pltpu.VMEM
    return pl.pallas_call(
        functools.partial(block_kernel, n, n_mp, zc, hp),
        out_shape=(
            jax.ShapeDtypeStruct((2, block, group), BF16),
            jax.ShapeDtypeStruct((chunks, 2, nc, keep, wide), BF16),
            jax.ShapeDtypeStruct((8, 128), F32),
        ),
        in_specs=[anywhere, anywhere, anywhere, pl.BlockSpec(memory_space=pltpu.SMEM), anywhere],
        out_specs=(anywhere, anywhere, vmem),
        scratch_shapes=[
            v((nc, length, rows), BF16),
            v((n_mp, zc, piece // zc, length), BF16),
            v((2 * n_mp, zc, piece // zc, length), BF16),
            v((2,) + weight.shape, BF16),
            v((length, group), BF16),
            v((group, length), BF16),
            v((2, block, group), BF16),
            v((block, group), BF16),
            v((2, group + 16, block), BF16),
            v((group, 128), F32),
            v((group, 128), F32),
            v((nc, chunks, 8, HD), F32),
            v((nc, 8, group), F32),
            v((n, imgs, 128), jnp.int32),
            v((rows, columns), BF16),
            v((keep, columns), BF16),
            v((keep, columns), F32),
            v((keep, keep), F32),
            v((keep, HD), F32),
            v((chunks, nc, keep, wide), F32),
            v((chunks, side, side, keep, wide), BF16),
            v((chunks, side, side, keep, wide), BF16),
            v((chunks, side, keep, wide), BF16),
            v((chunks, keep, wide), F32),
            v((chunks, side, keep, wide), BF16),
            v((chunks, 2, nc, keep, wide), BF16),
            v((8, 128), F32),
            v((n_mp, 8, 128), F32),
            v((n, 8, 128), F32),
            v((8, 128), F32),
            dma(), dma(), dma(),
            dma(n), dma(n),
            dma(side, side), dma(side, side),
            dma(n_mp, zc), dma(n_mp, zc), dma(n_mp, zc), dma(n_mp, zc),
            dma(n_mp, zc), dma(n_mp, zc), dma(zc),
            dma(n_mp, zc), dma(n_mp, zc),
            dma(), dma(), dma(),
            dma(nc), dma(nc), dma(nc), dma(nc),
            dma(), dma(),
            dma(chunks, side), dma(chunks, side),
            dma(chunks, side), dma(chunks, side),
            dma(chunks, side), dma(chunks, side),
            dma(chunks, side, side), dma(chunks, side, side),
            dma(chunks, side, side), dma(chunks, side, side),
            dma(n_mp), dma(n_mp), dma(n), dma(n),
            dma(chunks), dma(2),
        ],
        compiler_params=pltpu.CompilerParams(
            collective_id=0, has_side_effects=True, vmem_limit_bytes=VMEM_BYTES
        ),
    )(patches, embed, weight, counts, targets)


def weight_grad_kernel(left, right, loss_in, out, loss_out, stage, sem):
    chunks, _, _, wide = stage.shape
    both = jnp.concatenate([left[0], left[1]], axis=1)
    copies = []
    for k in range(chunks):
        value = fdot(both, right[k])
        for s in range(3):
            stage[k, s] = value[:, s * wide:(s + 1) * wide]
        copies.append(pltpu.make_async_copy(stage.at[k], out.at[:, :, pl.ds(k * wide, wide)], sem.at[k]))
        copies[-1].start()
    loss_out[0, 0] = loss_in[0, 0]
    for copy in copies:
        copy.wait()


def weight_grad_of(left, grads, loss):
    _, block, group = left.shape
    chunks, wide = grads.shape[0], grads.shape[-1] // 3
    right = grads.reshape(chunks, 2 * group, 3 * wide)
    vmem = pl.BlockSpec(memory_space=pltpu.VMEM)
    smem = pl.BlockSpec(memory_space=pltpu.SMEM)
    return pl.pallas_call(
        weight_grad_kernel,
        out_shape=(
            jax.ShapeDtypeStruct((3, block, chunks * wide), F32),
            jax.ShapeDtypeStruct((1, 1), F32),
        ),
        in_specs=[vmem, vmem, smem],
        out_specs=(pl.BlockSpec(memory_space=pl.ANY), smem),
        scratch_shapes=[
            pltpu.VMEM((chunks, 3, block, wide), F32),
            pltpu.SemaphoreType.DMA((chunks,)),
        ],
        compiler_params=pltpu.CompilerParams(vmem_limit_bytes=VMEM_BYTES),
    )(left, right, loss)


def local(n, n_mp, patches, embed_weight, project_weight, patch_counts, segment_ids, targets):
    del segment_ids
    left, grads, loss = run_block(
        patches.T, embed_weight, jnp.transpose(project_weight, (1, 0, 2)), patch_counts, targets, n, n_mp
    )
    weight_grad, loss = weight_grad_of(left, grads, loss)
    return (jnp.transpose(weight_grad, (1, 0, 2)), loss.reshape(()))


def solution(mesh):
    in_specs = (
        P("dp", None),
        P(("mp", "dp"), None),
        P("dp", None, "mp"),
        P("dp"),
        P("dp"),
        P("dp", "mp"),
    )
    out_specs = (P("dp", None, "mp"), P())
    return jax.shard_map(
        functools.partial(local, mesh.shape["dp"], mesh.shape["mp"]), mesh=mesh, in_specs=in_specs, out_specs=out_specs, check_vma=False)
```

```python
import functools
import math

import jax
import jax.numpy as jnp
from jax import lax
from jax.experimental import pallas as pl
from jax.experimental.pallas import tpu as pltpu
from jax.sharding import PartitionSpec as P

HD = 128
MESH = pl.DeviceIdType.MESH
VMEM_BYTES = 62 * 1024 * 1024
F32, BF16 = jnp.float32, jnp.bfloat16


def remote(src, dst, send_sem, recv_sem, device_id):
    return pltpu.make_async_remote_copy(
        src_ref=src, dst_ref=dst, send_sem=send_sem, recv_sem=recv_sem,
        device_id=device_id, device_id_type=MESH,
    )


def greet(n, n_mp, d, m):
    barrier = pltpu.get_barrier_semaphore()
    for i in range(1, n):
        pl.semaphore_signal(barrier, inc=1, device_id={"dp": lax.rem(d + i, n)}, device_id_type=MESH)
    for i in range(1, n_mp):
        pl.semaphore_signal(barrier, inc=1, device_id={"mp": lax.rem(m + i, n_mp)}, device_id_type=MESH)
    pl.semaphore_wait(barrier, n - 1 + n_mp - 1)


def grid_side(nc):
    side = math.isqrt(nc)
    assert side * side == nc
    return side


def fdot(a, b, dims=((1,), (0,))):
    return lax.dot_general(a, b, (dims, ((), ())), preferred_element_type=F32)


def layer_parts(x):
    center = x - jnp.mean(x, axis=-1, keepdims=True)
    scale = lax.rsqrt(jnp.mean(center * center, axis=-1, keepdims=True) + 1e-06)
    return center * scale, scale


def norm_grad(unit, scale, g):
    along = jnp.mean(g * unit, axis=-1, keepdims=True)
    return scale * (g - jnp.mean(g, axis=-1, keepdims=True) - unit * along)


def block_kernel(
    n, n_mp, zc, hp,
    patches, embed, weight, counts, targets,
    left, grads, loss,
    pall, zbuf, wp, wbuf, xt, xn, e, nrm, center_of, of_row, sums, stats, metas, town, ttail, tgt,
    allow, live, pf, sb, r1, s2b, raw, r2, gath, sq, zsq, psq, mine,
    w_sem, wx, wy, ms, mr, ps, pr, us, ur, vs, vr, es, er, el, fs, fr, ts, tr, tl,
    ss, sr, ks, kr, ns, nr, as_, ar, bs, br, gs, gr, hs, hr, cs, cr, zs, zr, qs, qr, os, ls,
):
    d, m = lax.axis_index("dp"), lax.axis_index("mp")
    core, chip = lax.rem(d, 2), d // 2
    partner = d + 1 - 2 * core
    nc = n // 2
    side = grid_side(nc)
    cx, cy = lax.rem(chip, side), chip // side
    rows = targets.shape[0]
    keep = rows * 3 // 4
    low = rows - keep
    group = nc * keep
    piece = embed.shape[0]
    part = piece // zc
    block = n_mp * piece
    span = n // (2 * n_mp)
    imgs = counts.shape[0]
    chunks = pf.shape[0]
    wide = hp * HD
    pair = lax.rem(d + n // 2, n)
    is_low = jnp.where(d < n // 2, 1, 0)

    def chip_at(h, u, v):
        dx = u * (1 - h) + v * h
        dy = u * h + v * (1 - h)
        return lax.rem(cy + dy + side, side) * side + lax.rem(cx + dx + side, side)

    def dev(c):
        return {"dp": 2 * c + core}

    w_own = pltpu.make_async_copy(weight, wbuf.at[core], w_sem)
    w_own.start()
    t_own = pltpu.make_async_copy(targets, town, tl)
    t_own.start()
    p_local = pltpu.make_async_copy(patches, pall.at[chip], ps.at[0, 0])
    p_local.start()
    cum = jnp.zeros((imgs, 128), jnp.int32)
    line = lax.broadcasted_iota(jnp.int32, (imgs, 128), 0)
    total = jnp.int32(0)
    for s in range(imgs):
        total = total + counts[s]
        cum = jnp.where(line == s, total, cum)
    metas[d] = cum

    greet(n, n_mp, d, m)

    def p_first(u):
        return remote(patches, pall.at[chip], ps.at[u, 0], pr.at[u, 0], dev(chip_at(core, u, 0)))

    def p_second(u, v):
        at = chip_at(core, -u, 0)
        src = patches if u == 0 else pall.at[at]
        return remote(src, pall.at[at], ps.at[u, v], pr.at[u, v], dev(chip_at(core, 0, v)))

    def m_copy(i):
        return remote(metas.at[d], metas.at[d], ms.at[i], mr.at[i], {"dp": lax.rem(d + i, n)})

    for u in range(1, side):
        p_first(u).start()
    for v in range(1, side):
        p_second(0, v).start()

    def z_copy(up, i, c):
        origin = m - i if up else m + i
        src = embed.at[pl.ds(c * part, part)] if i == 0 else zbuf.at[origin, c]
        send, recv = (us, ur) if up else (vs, vr)
        return remote(src, zbuf.at[origin, c], send.at[i, c], recv.at[i + 1, c], {"mp": m + 1 if up else m - 1})

    def z_wait(up, i, c):
        origin = m - i if up else m + i
        send, recv = (us, ur) if up else (vs, vr)
        remote(zbuf.at[origin, c], zbuf.at[origin, c], send.at[i, c], recv.at[i, c], {"mp": m - 1 if up else m + 1}).wait_recv()

    def z_has(up, i):
        return m - i >= 0 if up else m + i <= n_mp - 1

    def z_sends(up, i):
        return (m - i >= 0) & (m < n_mp - 1) if up else (m + i <= n_mp - 1) & (m > 0)

    slot = lax.rem(d, 2 * n_mp)
    rel_own = lax.rem(chip, n_mp)

    def owner(origin):
        return origin * span + d // (2 * n_mp)

    def e_copy(origin, src, c):
        return remote(src, wp.at[slot, c], es.at[origin, c], er.at[rel_own, c], dev(owner(origin)))

    def e_local(src, c):
        return pltpu.make_async_copy(src, wp.at[slot, c], el.at[c])

    def e_start(origin, own, c):
        src = embed.at[pl.ds(c * part, part)] if own else zbuf.at[origin, c]

        @pl.when(owner(origin) != chip)
        def _():
            e_copy(origin, src, c).start()

        @pl.when(owner(origin) == chip)
        def _():
            e_local(src, c).start()

    def z_own(c):
        for up in (True, False):
            @pl.when(z_sends(up, 0))
            def _():
                z_copy(up, 0, c).start()
        e_start(m, True, c)

    for c in range(min(2, zc)):
        z_own(c)
    for i in range(1, n):
        m_copy(i).start()

    w_swap = remote(weight, wbuf.at[core], wx, wy, {"dp": partner})
    w_swap.start()

    p_local.wait()

    def t_copy():
        return remote(town.at[pl.ds(low, keep)], ttail, ts, tr, {"dp": pair})

    t_own.wait()

    @pl.when(is_low == 1)
    def _():
        sq[...] = jnp.zeros_like(sq)

    @pl.when(is_low == 0)
    def _():
        sq[...] = jnp.zeros_like(sq)
        ttail[...] = jnp.zeros_like(ttail)

    def z_wave(w):
        for i in range(1, n_mp):
            c = w + 1 - i
            if 0 <= c < zc:
                for up in (True, False):
                    @pl.when(z_has(up, i))
                    def _():
                        z_wait(up, i, c)
                        if i < n_mp - 1:
                            @pl.when(z_sends(up, i))
                            def _():
                                z_copy(up, i, c).start()
                        e_start(m - i if up else m + i, False, c)
        if w + 2 < zc:
            z_own(w + 2)

    waves = zc + n_mp - 2
    for w in range(waves - 1):
        z_wave(w)
        if w == 1:
            for u in range(1, side):
                p_first(u).wait_recv()
                for v in range(1, side):
                    p_second(u, v).start()

    for v in range(1, side):
        for u in range(side):
            p_second(u, v).wait_recv()
    for i in range(1, n):
        m_copy(i).wait_recv()

    def ends(meta):
        fits = jnp.zeros((1, 1), jnp.int32)
        for s in range(imgs):
            at = meta[s:s + 1, 0:1]
            fits = jnp.maximum(fits, jnp.where(at <= keep, at, 0))
        return fits, meta[imgs - 1:imgs, 0:1]

    lane = lax.broadcasted_iota(jnp.int32, (1, group), 1)
    source = jnp.full((1, group), -1, jnp.int32)
    for j in range(nc // 2):
        far = j + nc // 2
        _, held = ends(metas[2 * j + core])
        fits, full = ends(metas[2 * far + core])
        r = lane - j * keep
        tail = fits + r - held
        at = jnp.where(r < held, j * rows + r, jnp.where(tail < full, far * rows + tail, -1))
        source = jnp.where((r >= 0) & (r < keep), at, source)
        r = lane - far * keep
        source = jnp.where((r >= 0) & (r < fits) & (r < keep), far * rows + r, source)
    picked = None
    for j in range(nc):
        place_of = lax.broadcasted_iota(jnp.int32, (rows, group), 0) + j * rows
        pick = jnp.where(place_of == source, 1.0, 0.0).astype(BF16)
        term = fdot(pall[j], pick)
        picked = term if picked is None else picked + term
    xt[...] = picked.astype(BF16)
    xn[...] = picked.astype(BF16).T
    for b in range(2):
        nrm[b, group:group + 16, :] = jnp.ones((16, block), BF16)

    fits_own, full_own = ends(metas[d])
    fits_far, full_far = ends(metas[pair])
    limit = is_low * full_own + (1 - is_low) * fits_own

    def place(shape, dim):
        r = lax.broadcasted_iota(jnp.int32, shape, dim)
        tail = fits_far + r - limit
        near = r < limit
        moved = (r >= limit) & (tail < full_far) & (is_low == 1)
        return r, tail, near, moved

    total_f = jnp.zeros((1, 1), jnp.int32)
    for i in range(n):
        total_f = total_f + metas[i][imgs - 1:imgs, 0:1]
    total_f = total_f.astype(F32)

    for w in range(waves - 1, waves):
        z_wave(w)

    base = n_mp * lax.rem(chip, span)

    def f_copy(i, c):
        q = 2 * i + core
        return remote(wp.at[q, c], wp.at[q, c], fs.at[i, c], fr.at[i, c], {"dp": partner})

    for c in range(zc):
        for i in range(n_mp):
            @pl.when(base + i == chip)
            def _():
                e_local(zbuf.at[0, c], c).wait()

            @pl.when(base + i != chip)
            def _():
                q = 2 * i + core
                remote(wp.at[q, c], wp.at[q, c], es.at[i, c], er.at[i, c], {"dp": partner}).wait_recv()

            f_copy(i, c).start()

    @pl.when(is_low == 0)
    def _():
        t_copy().start()

    per = 1 if 2 * piece % 128 == 0 else n_mp // 2
    lump = 2 * piece * per

    def pieces(i):
        return jnp.concatenate(
            [wp[2 * j + k, c] for j in range(i * per, (i + 1) * per) for k in range(2) for c in range(zc)], axis=0
        )

    def spot(i):
        return divmod(i * lump, block)

    for i in range(n_mp // per):
        for j in range(i * per, (i + 1) * per):
            for c in range(zc):
                f_copy(j, c).wait_recv()
        b, at = spot(i)
        nrm[b, 0:group, at:at + lump] = fdot(xn[...], pieces(i), ((1,), (1,))).astype(BF16)
    ones = jnp.ones((block, 128), BF16)
    about = (fdot(nrm[0, 0:group, :], ones) + fdot(nrm[1, 0:group, :], ones)) * (0.5 / block)
    center_of[...] = about
    w_own.wait()
    w_swap.wait_recv()

    def way(k):
        return lax.rem(k + core, 2)

    def a_copy(k, u):
        return remote(sb.at[k, u], r1.at[k, u], as_.at[k, u], ar.at[k, u], dev(chip_at(way(k), u, 0)))

    def b_copy(k, v):
        return remote(s2b.at[k, v], r2.at[k, v], bs.at[k, v], br.at[k, v], dev(chip_at(way(k), 0, v)))

    ahead = chunks - 1 if chunks > 2 else chunks

    def project(k, carry):
        acc = None
        for b in range(2):
            cols = jnp.concatenate(
                [wbuf[b, s, :, pl.ds(pl.multiple_of(k * wide, wide), wide)] for s in range(3)], axis=1
            )
            term = fdot(nrm[b], cols)
            acc = term if acc is None else acc + term
        for s in range(3 * hp):
            sums[0, k, s:s + 1, :] = acc[group:group + 1, s * HD:(s + 1) * HD]
        center = jnp.concatenate([center_of[...]] * (3 * hp), axis=1)
        pf[k] = (acc[0:group] - center * acc[group:group + 1]).reshape(nc, keep, 3 * wide)
        for u in range(1, side):
            for v in range(side):
                sb[k, u, v] = pf[k, chip_at(way(k), u, v)].astype(BF16)

            @pl.when(k < ahead)
            def _():
                a_copy(k, u).start()
        return carry

    lax.fori_loop(0, chunks, project, 0)

    def s_copy(i):
        return remote(stats.at[0], stats.at[i], ss.at[i], sr.at[i], dev(lax.rem(chip + i, nc)))

    def k_copy(i):
        return remote(sums.at[0], sums.at[i], ks.at[i], kr.at[i], dev(lax.rem(chip + i, nc)))

    for i in range(1, nc):
        k_copy(i).start()
    means, squares = [], []
    for i in range(n_mp // per):
        b, at = spot(i)
        value = fdot(pieces(i), xt[...]).astype(BF16)
        e[b, at:at + lump, :] = value
        value = value.astype(F32)
        mean = jnp.mean(value, axis=0, keepdims=True)
        center = value - mean
        means.append(mean)
        squares.append(jnp.sum(center * center, axis=0, keepdims=True))
    mean = sum(means) * (1.0 / len(means))
    square = sum(squares)
    for one in means:
        square = square + lump * ((one - mean) * (one - mean))
    stats[0, 0:1, :] = mean
    stats[0, 1:2, :] = square
    for i in range(1, nc):
        s_copy(i).start()

    @pl.when(is_low == 1)
    def _():
        t_copy().wait_recv()

    def ident(shape, dim):
        r, tail, near, moved = place(shape, dim)
        first = jnp.zeros(shape, jnp.int32)
        second = jnp.full(shape, imgs, jnp.int32)
        mine_, theirs = metas[d], metas[pair]
        for s in range(imgs):
            first = first + jnp.where(mine_[s:s + 1, 0:1] <= r, 1, 0)
            second = second + jnp.where(theirs[s:s + 1, 0:1] <= tail, 1, 0)
        return jnp.where(near, first, jnp.where(moved, second, -1))

    down, over = ident((keep, keep), 0), ident((keep, keep), 1)
    allow[...] = jnp.where((down == over) & (down >= 0), 1.0, 0.0)
    live[...] = jnp.where(ident((keep, HD), 0) >= 0, 1.0, 0.0)
    r, tail, near, moved = place((keep, rows), 0)
    col = lax.broadcasted_iota(jnp.int32, (keep, rows), 1)
    pick_own = jnp.where(near & (col == r), 1.0, 0.0).astype(BF16)
    r, tail, near, moved = place((keep, keep), 0)
    col = lax.broadcasted_iota(jnp.int32, (keep, keep), 1)
    pick_far = jnp.where(moved & (col == tail - low), 1.0, 0.0).astype(BF16)
    tgt[...] = fdot(pick_own, town[...]) + fdot(pick_far, ttail[...])

    def fold(k, carry):
        for u in range(1, side):
            a_copy(k, u).wait_recv()
        for v in range(1, side):
            value = pf[k, chip_at(way(k), 0, v)]
            for u in range(1, side):
                value = value + r1[k, u, v].astype(F32)
            s2b[k, v] = value.astype(BF16)
            b_copy(k, v).start()
        value = pf[k, chip]
        for u in range(1, side):
            value = value + r1[k, u, 0].astype(F32)
        raw[k] = value
        return carry

    fold(0, 0)
    for k in range(ahead, chunks):
        for u in range(1, side):
            a_copy(k, u).start()
    if ahead > 1:
        lax.fori_loop(1, ahead, fold, 0)

    for i in range(1, nc):
        s_copy(i).wait_recv()
    mean = sum(stats[i, 0:1, :] for i in range(nc)) * (1.0 / nc)
    square = jnp.zeros((1, group), F32)
    for i in range(nc):
        gap = stats[i, 0:1, :] - mean
        square = square + stats[i, 1:2, :] + (2.0 * block) * (gap * gap)
    scale = lax.rsqrt(square * (1.0 / (2.0 * block * nc)) + 1e-06)
    line = lax.broadcasted_iota(jnp.int32, (128, group), 0)
    both = jnp.where(line == 0, scale, 0.0)
    for i in range(nc):
        both = jnp.where(line == 1 + i, stats[i, 0:1, :] - mean, both)
    of_row[...] = both.T
    step = 384 if block % 384 == 0 else block
    for b in range(2):
        for at in range(0, block, step):
            value = (e[b, at:at + step, :].astype(F32) - mean) * scale
            e[b, at:at + step, :] = value.astype(BF16)
    n_copy = remote(e.at[1 - core], left.at[1], ns, nr, {"dp": partner})
    n_copy.start()
    for i in range(1, nc):
        k_copy(i).wait_recv()

    root = 1.0 / math.sqrt(HD)
    per_total = 1.0 / total_f

    def g_first(k, u):
        return remote(gath.at[k, chip], gath.at[k, chip], gs.at[k, u], gr.at[k, u], dev(chip_at(way(k), u, 0)))

    def g_second(k, u, v):
        at = chip_at(way(k), -u, 0)
        return remote(gath.at[k, at], gath.at[k, at], hs.at[k, u, v], hr.at[k, u, v], dev(chip_at(way(k), 0, v)))

    def g_across(k, u, v):
        at = chip_at(way(k), -u, -v)
        return remote(gath.at[k, at], grads.at[k, 1, at], cs.at[k, u, v], cr.at[k, u, v], {"dp": partner})

    def attend(k):
        for v in range(1, side):
            b_copy(k, v).wait_recv()
        mask, alive = allow[...], live[...]
        mine_rows = of_row[pl.ds(pl.multiple_of(chip * keep, keep), keep), :]
        row_scale = mine_rows[:, 0:1]
        gaps = [jnp.broadcast_to(mine_rows[:, 1 + i:2 + i], (keep, HD)) for i in range(nc)]
        error_sum = jnp.zeros((8, HD), F32)
        for h in range(hp):
            part_of = []
            for s in range(3):
                cols = slice(s * wide + h * HD, s * wide + (h + 1) * HD)
                value = raw[k, :, cols]
                for v in range(1, side):
                    value = value + r2[k, v, :, cols].astype(F32)
                for i in range(nc):
                    value = value + gaps[i] * sums[i, k, s * hp + h:s * hp + h + 1, :]
                part_of.append(value * row_scale)
            q_unit, q_scale = layer_parts(part_of[0])
            k_unit, k_scale = layer_parts(part_of[1])
            q_n, k_n, v_n = q_unit.astype(BF16), k_unit.astype(BF16), part_of[2].astype(BF16)
            scores = fdot(q_n, k_n, ((1,), (1,))) * root
            power = jnp.where(mask > 0.0, jnp.exp(scores), 0.0)
            below = jnp.sum(power, axis=-1, keepdims=True)
            below = jnp.where(below > 0.0, below, 1.0)
            weights = (power / below).astype(BF16)
            want = tgt[:, pl.ds(pl.multiple_of(k * wide + h * HD, HD), HD)]
            error = jnp.where(alive > 0.0, fdot(weights, v_n) - want, 0.0)
            error_sum = error_sum + jnp.sum((error * error).reshape(keep // 8, 8, HD), axis=0)
            out_grad = (error * per_total).astype(BF16)
            prob_grad = fdot(out_grad, v_n, ((1,), (1,)))
            value_grad = fdot(weights, out_grad, ((0,), (0,)))
            weight_f = weights.astype(F32)
            score_grad = (
                weight_f * (prob_grad - jnp.sum(prob_grad * weight_f, axis=-1, keepdims=True)) * root
            ).astype(BF16)
            q_grad = norm_grad(q_unit, q_scale, fdot(score_grad, k_n))
            k_grad = norm_grad(k_unit, k_scale, fdot(score_grad, q_n, ((0,), (0,))))
            for s, value in enumerate((q_grad, k_grad, value_grad)):
                gath[k, chip, :, s * wide + h * HD:s * wide + (h + 1) * HD] = value.astype(BF16)
        sq[...] += error_sum
        for u in range(1, side):
            g_first(k, u).start()
        for v in range(1, side):
            g_second(k, 0, v).start()
        g_across(k, 0, 0).start()

    def o_copy(k):
        return pltpu.make_async_copy(gath.at[k], grads.at[k, 0], os.at[k])

    def relay(k):
        for u in range(1, side):
            g_first(k, u).wait_recv()
            for v in range(1, side):
                g_second(k, u, v).start()
            g_across(k, u, 0).start()

    def cross(k):
        for u in range(side):
            for v in range(1, side):
                g_second(k, u, v).wait_recv()
                g_across(k, u, v).start()
        o_copy(k).start()

    def finish(k):
        for u in range(side):
            for v in range(side):
                g_across(k, u, v).wait_recv()

    left_copy = pltpu.make_async_copy(e.at[core], left.at[0], ls)
    left_copy.start()

    def y_copy(i):
        return remote(sq, zsq.at[i], zs.at[i], zr.at[i], {"mp": lax.rem(m + i, n_mp)})

    def l_copy(i):
        return remote(mine, psq.at[i], qs.at[i], qr.at[i], {"dp": lax.rem(d + i, n)})

    def flow(i, carry):
        @pl.when(i < chunks)
        def _():
            attend(i)

        @pl.when((i >= 0) & (i < chunks - ahead))
        def _():
            fold(ahead + i, 0)

        @pl.when(i == chunks - 1)
        def _():
            for j in range(1, n_mp):
                y_copy(j).start()

        @pl.when((i >= 1) & (i <= chunks))
        def _():
            relay(i - 1)

        @pl.when(i == chunks)
        def _():
            value = sq[...]
            for j in range(1, n_mp):
                y_copy(j).wait_recv()
                value = value + zsq[j]
            mine[...] = value
            for j in range(1, n):
                l_copy(j).start()

        @pl.when((i >= 2) & (i <= chunks + 1))
        def _():
            cross(i - 2)

        @pl.when(i >= 3)
        def _():
            finish(i - 3)

        return carry

    lax.fori_loop(0, chunks + 2, flow, 0)

    finish(chunks - 1)
    value = mine[...]
    for i in range(1, n):
        l_copy(i).wait_recv()
        value = value + psq[i]
    value = jnp.sum(jnp.sum(value, axis=1, keepdims=True), axis=0, keepdims=True)
    loss[...] = jnp.broadcast_to(value * (0.5 * per_total), loss.shape)

    for u in range(1, side):
        p_first(u).wait_send()
    for v in range(1, side):
        for u in range(side):
            p_second(u, v).wait_send()
    for i in range(1, n):
        m_copy(i).wait_send()
        l_copy(i).wait_send()
    for i in range(1, n_mp):
        y_copy(i).wait_send()
    for c in range(zc):
        for i in range(n_mp - 1):
            for up in (True, False):
                @pl.when(z_sends(up, i))
                def _():
                    z_copy(up, i, c).wait_send()
        for i in range(n_mp):
            f_copy(i, c).wait_send()

            @pl.when(owner(i) != chip)
            def _():
                e_copy(i, zbuf.at[i, c], c).wait_send()

    @pl.when(is_low == 0)
    def _():
        t_copy().wait_send()

    w_swap.wait_send()
    n_copy.wait_send()
    n_copy.wait_recv()
    left_copy.wait()
    for i in range(1, nc):
        s_copy(i).wait_send()
        k_copy(i).wait_send()

    def drain(k, carry):
        for u in range(1, side):
            a_copy(k, u).wait_send()
            g_first(k, u).wait_send()
        for v in range(1, side):
            b_copy(k, v).wait_send()
            for u in range(side):
                g_second(k, u, v).wait_send()
        for u in range(side):
            for v in range(side):
                g_across(k, u, v).wait_send()
        o_copy(k).wait()
        return carry

    lax.fori_loop(0, chunks, drain, 0)


def run_block(patches, embed, weight, counts, targets, n, n_mp):
    length, rows = patches.shape
    piece = embed.shape[0]
    columns = weight.shape[2]
    heads = columns // HD
    nc = n // 2
    side = grid_side(nc)
    keep = rows * 3 // 4
    group = nc * keep
    block = n_mp * piece
    imgs = counts.shape[0]
    assert n % (2 * n_mp) == 0 and block == weight.shape[1]
    zc = 4 if piece % 64 == 0 else 1
    hp = 2 if heads % 2 == 0 else 1
    chunks = heads // hp
    wide = 3 * hp * HD
    dma = lambda *k: pltpu.SemaphoreType.DMA(k) if k else pltpu.SemaphoreType.DMA
    anywhere = pl.BlockSpec(memory_space=pl.ANY)
    vmem = pl.BlockSpec(memory_space=pltpu.VMEM)
    v = pltpu.VMEM
    return pl.pallas_call(
        functools.partial(block_kernel, n, n_mp, zc, hp),
        out_shape=(
            jax.ShapeDtypeStruct((2, block, group), BF16),
            jax.ShapeDtypeStruct((chunks, 2, nc, keep, wide), BF16),
            jax.ShapeDtypeStruct((8, 128), F32),
        ),
        in_specs=[anywhere, anywhere, anywhere, pl.BlockSpec(memory_space=pltpu.SMEM), anywhere],
        out_specs=(anywhere, anywhere, vmem),
        scratch_shapes=[
            v((nc, length, rows), BF16),
            v((n_mp, zc, piece // zc, length), BF16),
            v((2 * n_mp, zc, piece // zc, length), BF16),
            v((2,) + weight.shape, BF16),
            v((length, group), BF16),
            v((group, length), BF16),
            v((2, block, group), BF16),
            v((2, group + 16, block), BF16),
            v((group, 128), F32),
            v((group, 128), F32),
            v((nc, chunks, 8, HD), F32),
            v((nc, 8, group), F32),
            v((n, imgs, 128), jnp.int32),
            v((rows, columns), BF16),
            v((keep, columns), BF16),
            v((keep, columns), F32),
            v((keep, keep), F32),
            v((keep, HD), F32),
            v((chunks, nc, keep, wide), F32),
            v((chunks, side, side, keep, wide), BF16),
            v((chunks, side, side, keep, wide), BF16),
            v((chunks, side, keep, wide), BF16),
            v((chunks, keep, wide), F32),
            v((chunks, side, keep, wide), BF16),
            v((chunks, nc, keep, wide), BF16),
            v((8, 128), F32),
            v((n_mp, 8, 128), F32),
            v((n, 8, 128), F32),
            v((8, 128), F32),
            dma(), dma(), dma(),
            dma(n), dma(n),
            dma(side, side), dma(side, side),
            dma(n_mp, zc), dma(n_mp, zc), dma(n_mp, zc), dma(n_mp, zc),
            dma(n_mp, zc), dma(n_mp, zc), dma(zc),
            dma(n_mp, zc), dma(n_mp, zc),
            dma(), dma(), dma(),
            dma(nc), dma(nc), dma(nc), dma(nc),
            dma(), dma(),
            dma(chunks, side), dma(chunks, side),
            dma(chunks, side), dma(chunks, side),
            dma(chunks, side), dma(chunks, side),
            dma(chunks, side, side), dma(chunks, side, side),
            dma(chunks, side, side), dma(chunks, side, side),
            dma(n_mp), dma(n_mp), dma(n), dma(n),
            dma(chunks), dma(),
        ],
        compiler_params=pltpu.CompilerParams(
            collective_id=0, has_side_effects=True, vmem_limit_bytes=VMEM_BYTES
        ),
    )(patches, embed, weight, counts, targets)


def weight_grad_kernel(left, right, loss_in, out, loss_out, stage, sem):
    chunks, _, _, wide = stage.shape
    both = jnp.concatenate([left[0], left[1]], axis=1)
    copies = []
    for k in range(chunks):
        value = fdot(both, right[k])
        for s in range(3):
            stage[k, s] = value[:, s * wide:(s + 1) * wide]
        copies.append(pltpu.make_async_copy(stage.at[k], out.at[:, :, pl.ds(k * wide, wide)], sem.at[k]))
        copies[-1].start()
    loss_out[0, 0] = loss_in[0, 0]
    for copy in copies:
        copy.wait()


def weight_grad_of(left, grads, loss):
    _, block, group = left.shape
    chunks, wide = grads.shape[0], grads.shape[-1] // 3
    right = grads.reshape(chunks, 2 * group, 3 * wide)
    vmem = pl.BlockSpec(memory_space=pltpu.VMEM)
    smem = pl.BlockSpec(memory_space=pltpu.SMEM)
    return pl.pallas_call(
        weight_grad_kernel,
        out_shape=(
            jax.ShapeDtypeStruct((3, block, chunks * wide), F32),
            jax.ShapeDtypeStruct((1, 1), F32),
        ),
        in_specs=[vmem, vmem, smem],
        out_specs=(pl.BlockSpec(memory_space=pl.ANY), smem),
        scratch_shapes=[
            pltpu.VMEM((chunks, 3, block, wide), F32),
            pltpu.SemaphoreType.DMA((chunks,)),
        ],
        compiler_params=pltpu.CompilerParams(vmem_limit_bytes=VMEM_BYTES),
    )(left, right, loss)


def local(n, n_mp, patches, embed_weight, project_weight, patch_counts, segment_ids, targets):
    del segment_ids
    left, grads, loss = run_block(
        patches.T, embed_weight, jnp.transpose(project_weight, (1, 0, 2)), patch_counts, targets, n, n_mp
    )
    weight_grad, loss = weight_grad_of(left, grads, loss)
    return (jnp.transpose(weight_grad, (1, 0, 2)), loss.reshape(()))


def solution(mesh):
    in_specs = (
        P("dp", None),
        P(("mp", "dp"), None),
        P("dp", None, "mp"),
        P("dp"),
        P("dp"),
        P("dp", "mp"),
    )
    out_specs = (P("dp", None, "mp"), P())
    return jax.shard_map(
        functools.partial(local, mesh.shape["dp"], mesh.shape["mp"]), mesh=mesh, in_specs=in_specs, out_specs=out_specs, check_vma=False)
```

```python
import functools
import math

import jax
import jax.numpy as jnp
from jax import lax
from jax.experimental import pallas as pl
from jax.experimental.pallas import tpu as pltpu
from jax.sharding import PartitionSpec as P

HD = 128
MESH = pl.DeviceIdType.MESH
VMEM_BYTES = 62 * 1024 * 1024
F32, BF16 = jnp.float32, jnp.bfloat16


def remote(src, dst, send_sem, recv_sem, device_id):
    return pltpu.make_async_remote_copy(
        src_ref=src, dst_ref=dst, send_sem=send_sem, recv_sem=recv_sem,
        device_id=device_id, device_id_type=MESH,
    )


def greet(n, n_mp, d, m):
    barrier = pltpu.get_barrier_semaphore()
    for i in range(1, n):
        pl.semaphore_signal(barrier, inc=1, device_id={"dp": lax.rem(d + i, n)}, device_id_type=MESH)
    for i in range(1, n_mp):
        pl.semaphore_signal(barrier, inc=1, device_id={"mp": lax.rem(m + i, n_mp)}, device_id_type=MESH)
    pl.semaphore_wait(barrier, n - 1 + n_mp - 1)


def grid_side(nc):
    side = math.isqrt(nc)
    assert side * side == nc
    return side


def fdot(a, b, dims=((1,), (0,))):
    return lax.dot_general(a, b, (dims, ((), ())), preferred_element_type=F32)


def layer_parts(x):
    center = x - jnp.mean(x, axis=-1, keepdims=True)
    scale = lax.rsqrt(jnp.mean(center * center, axis=-1, keepdims=True) + 1e-06)
    return center * scale, scale


def norm_grad(unit, scale, g):
    along = jnp.mean(g * unit, axis=-1, keepdims=True)
    return scale * (g - jnp.mean(g, axis=-1, keepdims=True) - unit * along)


def block_kernel(
    n, n_mp, zc, hp,
    patches, embed, weight, counts, targets,
    left, grads, loss,
    pall, zbuf, wp, wbuf, xt, xn, e, nrm, center_of, of_row, sums, stats, metas, town, ttail, tgt,
    allow, live, pf, sb, r1, s2b, raw, r2, gath, sq, zsq, psq, mine,
    w_sem, wx, wy, ms, mr, ps, pr, us, ur, vs, vr, es, er, el, fs, fr, ts, tr, tl,
    ss, sr, ks, kr, ns, nr, as_, ar, bs, br, gs, gr, hs, hr, cs, cr, zs, zr, qs, qr, os, ls,
):
    d, m = lax.axis_index("dp"), lax.axis_index("mp")
    core, chip = lax.rem(d, 2), d // 2
    partner = d + 1 - 2 * core
    nc = n // 2
    side = grid_side(nc)
    cx, cy = lax.rem(chip, side), chip // side
    rows = targets.shape[0]
    keep = rows * 3 // 4
    low = rows - keep
    group = nc * keep
    piece = embed.shape[0]
    part = piece // zc
    block = n_mp * piece
    span = n // (2 * n_mp)
    imgs = counts.shape[0]
    chunks = pf.shape[0]
    wide = hp * HD
    pair = lax.rem(d + n // 2, n)
    is_low = jnp.where(d < n // 2, 1, 0)

    def chip_at(h, u, v):
        dx = u * (1 - h) + v * h
        dy = u * h + v * (1 - h)
        return lax.rem(cy + dy + side, side) * side + lax.rem(cx + dx + side, side)

    def dev(c):
        return {"dp": 2 * c + core}

    w_own = pltpu.make_async_copy(weight, wbuf.at[core], w_sem)
    w_own.start()
    t_own = pltpu.make_async_copy(targets, town, tl)
    t_own.start()
    p_local = pltpu.make_async_copy(patches, pall.at[chip], ps.at[0, 0])
    p_local.start()
    cum = jnp.zeros((imgs, 128), jnp.int32)
    line = lax.broadcasted_iota(jnp.int32, (imgs, 128), 0)
    total = jnp.int32(0)
    for s in range(imgs):
        total = total + counts[s]
        cum = jnp.where(line == s, total, cum)
    metas[d] = cum

    greet(n, n_mp, d, m)

    def p_first(u):
        return remote(patches, pall.at[chip], ps.at[u, 0], pr.at[u, 0], dev(chip_at(core, u, 0)))

    def p_second(u, v):
        at = chip_at(core, -u, 0)
        src = patches if u == 0 else pall.at[at]
        return remote(src, pall.at[at], ps.at[u, v], pr.at[u, v], dev(chip_at(core, 0, v)))

    def m_copy(i):
        return remote(metas.at[d], metas.at[d], ms.at[i], mr.at[i], {"dp": lax.rem(d + i, n)})

    for u in range(1, side):
        p_first(u).start()
    for v in range(1, side):
        p_second(0, v).start()

    def z_copy(up, i, c):
        origin = m - i if up else m + i
        src = embed.at[pl.ds(c * part, part)] if i == 0 else zbuf.at[origin, c]
        send, recv = (us, ur) if up else (vs, vr)
        return remote(src, zbuf.at[origin, c], send.at[i, c], recv.at[i + 1, c], {"mp": m + 1 if up else m - 1})

    def z_wait(up, i, c):
        origin = m - i if up else m + i
        send, recv = (us, ur) if up else (vs, vr)
        remote(zbuf.at[origin, c], zbuf.at[origin, c], send.at[i, c], recv.at[i, c], {"mp": m - 1 if up else m + 1}).wait_recv()

    def z_has(up, i):
        return m - i >= 0 if up else m + i <= n_mp - 1

    def z_sends(up, i):
        return (m - i >= 0) & (m < n_mp - 1) if up else (m + i <= n_mp - 1) & (m > 0)

    slot = lax.rem(d, 2 * n_mp)
    rel_own = lax.rem(chip, n_mp)

    def owner(origin):
        return origin * span + d // (2 * n_mp)

    def e_copy(origin, src, c):
        return remote(src, wp.at[slot, c], es.at[origin, c], er.at[rel_own, c], dev(owner(origin)))

    def e_local(src, c):
        return pltpu.make_async_copy(src, wp.at[slot, c], el.at[c])

    def e_start(origin, own, c):
        src = embed.at[pl.ds(c * part, part)] if own else zbuf.at[origin, c]

        @pl.when(owner(origin) != chip)
        def _():
            e_copy(origin, src, c).start()

        @pl.when(owner(origin) == chip)
        def _():
            e_local(src, c).start()

    def z_own(c):
        for up in (True, False):
            @pl.when(z_sends(up, 0))
            def _():
                z_copy(up, 0, c).start()
        e_start(m, True, c)

    for c in range(min(2, zc)):
        z_own(c)
    for i in range(1, n):
        m_copy(i).start()

    w_swap = remote(weight, wbuf.at[core], wx, wy, {"dp": partner})
    w_swap.start()

    p_local.wait()

    def t_copy():
        return remote(town.at[pl.ds(low, keep)], ttail, ts, tr, {"dp": pair})

    t_own.wait()

    @pl.when(is_low == 1)
    def _():
        sq[...] = jnp.zeros_like(sq)

    @pl.when(is_low == 0)
    def _():
        sq[...] = jnp.zeros_like(sq)
        ttail[...] = jnp.zeros_like(ttail)

    def z_wave(w):
        for i in range(1, n_mp):
            c = w + 1 - i
            if 0 <= c < zc:
                for up in (True, False):
                    @pl.when(z_has(up, i))
                    def _():
                        z_wait(up, i, c)
                        if i < n_mp - 1:
                            @pl.when(z_sends(up, i))
                            def _():
                                z_copy(up, i, c).start()
                        e_start(m - i if up else m + i, False, c)
        if w + 2 < zc:
            z_own(w + 2)

    waves = zc + n_mp - 2
    for w in range(waves - 1):
        z_wave(w)
        if w == 1:
            for u in range(1, side):
                p_first(u).wait_recv()
                for v in range(1, side):
                    p_second(u, v).start()

    for v in range(1, side):
        for u in range(side):
            p_second(u, v).wait_recv()
    for i in range(1, n):
        m_copy(i).wait_recv()

    def ends(meta):
        fits = jnp.zeros((1, 1), jnp.int32)
        for s in range(imgs):
            at = meta[s:s + 1, 0:1]
            fits = jnp.maximum(fits, jnp.where(at <= keep, at, 0))
        return fits, meta[imgs - 1:imgs, 0:1]

    lane = lax.broadcasted_iota(jnp.int32, (1, group), 1)
    source = jnp.full((1, group), -1, jnp.int32)
    for j in range(nc // 2):
        far = j + nc // 2
        _, held = ends(metas[2 * j + core])
        fits, full = ends(metas[2 * far + core])
        r = lane - j * keep
        tail = fits + r - held
        at = jnp.where(r < held, j * rows + r, jnp.where(tail < full, far * rows + tail, -1))
        source = jnp.where((r >= 0) & (r < keep), at, source)
        r = lane - far * keep
        source = jnp.where((r >= 0) & (r < fits) & (r < keep), far * rows + r, source)
    picked = None
    for j in range(nc):
        place_of = lax.broadcasted_iota(jnp.int32, (rows, group), 0) + j * rows
        pick = jnp.where(place_of == source, 1.0, 0.0).astype(BF16)
        term = fdot(pall[j], pick)
        picked = term if picked is None else picked + term
    xt[...] = picked.astype(BF16)
    xn[...] = picked.astype(BF16).T
    for b in range(2):
        nrm[b, group:group + 16, :] = jnp.ones((16, block), BF16)

    fits_own, full_own = ends(metas[d])
    fits_far, full_far = ends(metas[pair])
    limit = is_low * full_own + (1 - is_low) * fits_own

    def place(shape, dim):
        r = lax.broadcasted_iota(jnp.int32, shape, dim)
        tail = fits_far + r - limit
        near = r < limit
        moved = (r >= limit) & (tail < full_far) & (is_low == 1)
        return r, tail, near, moved

    total_f = jnp.zeros((1, 1), jnp.int32)
    for i in range(n):
        total_f = total_f + metas[i][imgs - 1:imgs, 0:1]
    total_f = total_f.astype(F32)

    for w in range(waves - 1, waves):
        z_wave(w)

    base = n_mp * lax.rem(chip, span)

    def f_copy(i, c):
        q = 2 * i + core
        return remote(wp.at[q, c], wp.at[q, c], fs.at[i, c], fr.at[i, c], {"dp": partner})

    for c in range(zc):
        for i in range(n_mp):
            @pl.when(base + i == chip)
            def _():
                e_local(zbuf.at[0, c], c).wait()

            @pl.when(base + i != chip)
            def _():
                q = 2 * i + core
                remote(wp.at[q, c], wp.at[q, c], es.at[i, c], er.at[i, c], {"dp": partner}).wait_recv()

            f_copy(i, c).start()

    @pl.when(is_low == 0)
    def _():
        t_copy().start()

    per = 1 if 2 * piece % 128 == 0 else n_mp // 2
    lump = 2 * piece * per

    def pieces(i):
        return jnp.concatenate(
            [wp[2 * j + k, c] for j in range(i * per, (i + 1) * per) for k in range(2) for c in range(zc)], axis=0
        )

    def spot(i):
        return divmod(i * lump, block)

    for i in range(n_mp // per):
        for j in range(i * per, (i + 1) * per):
            for c in range(zc):
                f_copy(j, c).wait_recv()
        b, at = spot(i)
        nrm[b, 0:group, at:at + lump] = fdot(xn[...], pieces(i), ((1,), (1,))).astype(BF16)
    ones = jnp.ones((block, 128), BF16)
    about = (fdot(nrm[0, 0:group, :], ones) + fdot(nrm[1, 0:group, :], ones)) * (0.5 / block)
    center_of[...] = about
    w_own.wait()
    w_swap.wait_recv()

    def way(k):
        return lax.rem(k + core, 2)

    def a_copy(k, u):
        return remote(sb.at[k, u], r1.at[k, u], as_.at[k, u], ar.at[k, u], dev(chip_at(way(k), u, 0)))

    def b_copy(k, v):
        return remote(s2b.at[k, v], r2.at[k, v], bs.at[k, v], br.at[k, v], dev(chip_at(way(k), 0, v)))

    ahead = chunks - 1 if chunks > 2 else chunks

    def project(k, carry):
        acc = None
        for b in range(2):
            cols = jnp.concatenate(
                [wbuf[b, s, :, pl.ds(pl.multiple_of(k * wide, wide), wide)] for s in range(3)], axis=1
            )
            term = fdot(nrm[b], cols)
            acc = term if acc is None else acc + term
        for s in range(3 * hp):
            sums[0, k, s:s + 1, :] = acc[group:group + 1, s * HD:(s + 1) * HD]
        center = jnp.concatenate([center_of[...]] * (3 * hp), axis=1)
        pf[k] = (acc[0:group] - center * acc[group:group + 1]).reshape(nc, keep, 3 * wide)
        for u in range(1, side):
            for v in range(side):
                sb[k, u, v] = pf[k, chip_at(way(k), u, v)].astype(BF16)

            @pl.when(k < ahead)
            def _():
                a_copy(k, u).start()
        return carry

    lax.fori_loop(0, chunks, project, 0)

    def s_copy(i):
        return remote(stats.at[0], stats.at[i], ss.at[i], sr.at[i], dev(lax.rem(chip + i, nc)))

    def k_copy(i):
        return remote(sums.at[0], sums.at[i], ks.at[i], kr.at[i], dev(lax.rem(chip + i, nc)))

    for i in range(1, nc):
        k_copy(i).start()
    means, squares = [], []
    for i in range(n_mp // per):
        b, at = spot(i)
        value = fdot(pieces(i), xt[...]).astype(BF16)
        e[b, at:at + lump, :] = value
        value = value.astype(F32)
        mean = jnp.mean(value, axis=0, keepdims=True)
        center = value - mean
        means.append(mean)
        squares.append(jnp.sum(center * center, axis=0, keepdims=True))
    mean = sum(means) * (1.0 / len(means))
    square = sum(squares)
    for one in means:
        square = square + lump * ((one - mean) * (one - mean))
    stats[0, 0:1, :] = mean
    stats[0, 1:2, :] = square
    for i in range(1, nc):
        s_copy(i).start()

    def fold(k, carry):
        for u in range(1, side):
            a_copy(k, u).wait_recv()
        for v in range(1, side):
            value = pf[k, chip_at(way(k), 0, v)]
            for u in range(1, side):
                value = value + r1[k, u, v].astype(F32)
            s2b[k, v] = value.astype(BF16)
            b_copy(k, v).start()
        value = pf[k, chip]
        for u in range(1, side):
            value = value + r1[k, u, 0].astype(F32)
        raw[k] = value
        return carry

    fold(0, 0)
    for k in range(ahead, chunks):
        for u in range(1, side):
            a_copy(k, u).start()
    if ahead > 1:
        lax.fori_loop(1, ahead, fold, 0)

    @pl.when(is_low == 1)
    def _():
        t_copy().wait_recv()

    def ident(shape, dim):
        r, tail, near, moved = place(shape, dim)
        first = jnp.zeros(shape, jnp.int32)
        second = jnp.full(shape, imgs, jnp.int32)
        mine_, theirs = metas[d], metas[pair]
        for s in range(imgs):
            first = first + jnp.where(mine_[s:s + 1, 0:1] <= r, 1, 0)
            second = second + jnp.where(theirs[s:s + 1, 0:1] <= tail, 1, 0)
        return jnp.where(near, first, jnp.where(moved, second, -1))

    down, over = ident((keep, keep), 0), ident((keep, keep), 1)
    allow[...] = jnp.where((down == over) & (down >= 0), 1.0, 0.0)
    live[...] = jnp.where(ident((keep, HD), 0) >= 0, 1.0, 0.0)
    r, tail, near, moved = place((keep, rows), 0)
    col = lax.broadcasted_iota(jnp.int32, (keep, rows), 1)
    pick_own = jnp.where(near & (col == r), 1.0, 0.0).astype(BF16)
    r, tail, near, moved = place((keep, keep), 0)
    col = lax.broadcasted_iota(jnp.int32, (keep, keep), 1)
    pick_far = jnp.where(moved & (col == tail - low), 1.0, 0.0).astype(BF16)
    tgt[...] = fdot(pick_own, town[...]) + fdot(pick_far, ttail[...])

    for i in range(1, nc):
        s_copy(i).wait_recv()
    mean = sum(stats[i, 0:1, :] for i in range(nc)) * (1.0 / nc)
    square = jnp.zeros((1, group), F32)
    for i in range(nc):
        gap = stats[i, 0:1, :] - mean
        square = square + stats[i, 1:2, :] + (2.0 * block) * (gap * gap)
    scale = lax.rsqrt(square * (1.0 / (2.0 * block * nc)) + 1e-06)
    line = lax.broadcasted_iota(jnp.int32, (128, group), 0)
    both = jnp.where(line == 0, scale, 0.0)
    for i in range(nc):
        both = jnp.where(line == 1 + i, stats[i, 0:1, :] - mean, both)
    of_row[...] = both.T
    step = 384 if block % 384 == 0 else block
    n_copy = remote(e.at[1 - core], left.at[1], ns, nr, {"dp": partner})
    left_copy = pltpu.make_async_copy(e.at[core], left.at[0], ls)

    def normalise():
        for b in range(2):
            for at in range(0, block, step):
                value = (e[b, at:at + step, :].astype(F32) - mean) * scale
                e[b, at:at + step, :] = value.astype(BF16)
        n_copy.start()
        left_copy.start()

    for i in range(1, nc):
        k_copy(i).wait_recv()

    root = 1.0 / math.sqrt(HD)
    per_total = 1.0 / total_f

    def g_first(k, u):
        return remote(gath.at[k, chip], gath.at[k, chip], gs.at[k, u], gr.at[k, u], dev(chip_at(way(k), u, 0)))

    def g_second(k, u, v):
        at = chip_at(way(k), -u, 0)
        return remote(gath.at[k, at], gath.at[k, at], hs.at[k, u, v], hr.at[k, u, v], dev(chip_at(way(k), 0, v)))

    def g_across(k, u, v):
        at = chip_at(way(k), -u, -v)
        return remote(gath.at[k, at], grads.at[k, 1, at], cs.at[k, u, v], cr.at[k, u, v], {"dp": partner})

    def attend(k):
        for v in range(1, side):
            b_copy(k, v).wait_recv()
        mask, alive = allow[...], live[...]
        mine_rows = of_row[pl.ds(pl.multiple_of(chip * keep, keep), keep), :]
        row_scale = mine_rows[:, 0:1]
        gaps = [jnp.broadcast_to(mine_rows[:, 1 + i:2 + i], (keep, HD)) for i in range(nc)]
        error_sum = jnp.zeros((8, HD), F32)
        for h in range(hp):
            part_of = []
            for s in range(3):
                cols = slice(s * wide + h * HD, s * wide + (h + 1) * HD)
                value = raw[k, :, cols]
                for v in range(1, side):
                    value = value + r2[k, v, :, cols].astype(F32)
                for i in range(nc):
                    value = value + gaps[i] * sums[i, k, s * hp + h:s * hp + h + 1, :]
                part_of.append(value * row_scale)
            q_unit, q_scale = layer_parts(part_of[0])
            k_unit, k_scale = layer_parts(part_of[1])
            q_n, k_n, v_n = q_unit.astype(BF16), k_unit.astype(BF16), part_of[2].astype(BF16)
            scores = fdot(q_n, k_n, ((1,), (1,))) * root
            power = jnp.where(mask > 0.0, jnp.exp(scores), 0.0)
            below = jnp.sum(power, axis=-1, keepdims=True)
            below = jnp.where(below > 0.0, below, 1.0)
            weights = (power / below).astype(BF16)
            want = tgt[:, pl.ds(pl.multiple_of(k * wide + h * HD, HD), HD)]
            error = jnp.where(alive > 0.0, fdot(weights, v_n) - want, 0.0)
            error_sum = error_sum + jnp.sum((error * error).reshape(keep // 8, 8, HD), axis=0)
            out_grad = (error * per_total).astype(BF16)
            prob_grad = fdot(out_grad, v_n, ((1,), (1,)))
            value_grad = fdot(weights, out_grad, ((0,), (0,)))
            weight_f = weights.astype(F32)
            score_grad = (
                weight_f * (prob_grad - jnp.sum(prob_grad * weight_f, axis=-1, keepdims=True)) * root
            ).astype(BF16)
            q_grad = norm_grad(q_unit, q_scale, fdot(score_grad, k_n))
            k_grad = norm_grad(k_unit, k_scale, fdot(score_grad, q_n, ((0,), (0,))))
            for s, value in enumerate((q_grad, k_grad, value_grad)):
                gath[k, chip, :, s * wide + h * HD:s * wide + (h + 1) * HD] = value.astype(BF16)
        sq[...] += error_sum
        for u in range(1, side):
            g_first(k, u).start()
        for v in range(1, side):
            g_second(k, 0, v).start()
        g_across(k, 0, 0).start()

    def o_copy(k):
        return pltpu.make_async_copy(gath.at[k], grads.at[k, 0], os.at[k])

    def relay(k):
        for u in range(1, side):
            g_first(k, u).wait_recv()
            for v in range(1, side):
                g_second(k, u, v).start()
            g_across(k, u, 0).start()

    def cross(k):
        for u in range(side):
            for v in range(1, side):
                g_second(k, u, v).wait_recv()
                g_across(k, u, v).start()
        o_copy(k).start()

    def finish(k):
        for u in range(side):
            for v in range(side):
                g_across(k, u, v).wait_recv()


    def y_copy(i):
        return remote(sq, zsq.at[i], zs.at[i], zr.at[i], {"mp": lax.rem(m + i, n_mp)})

    def l_copy(i):
        return remote(mine, psq.at[i], qs.at[i], qr.at[i], {"dp": lax.rem(d + i, n)})

    def flow(i, carry):
        @pl.when(i < chunks)
        def _():
            attend(i)

        @pl.when((i >= 0) & (i < chunks - ahead))
        def _():
            fold(ahead + i, 0)

        @pl.when(i == chunks - 1)
        def _():
            for j in range(1, n_mp):
                y_copy(j).start()

        @pl.when((i >= 1) & (i <= chunks))
        def _():
            relay(i - 1)

        @pl.when(i == chunks)
        def _():
            normalise()

        @pl.when(i == chunks)
        def _():
            value = sq[...]
            for j in range(1, n_mp):
                y_copy(j).wait_recv()
                value = value + zsq[j]
            mine[...] = value
            for j in range(1, n):
                l_copy(j).start()

        @pl.when((i >= 2) & (i <= chunks + 1))
        def _():
            cross(i - 2)

        @pl.when(i >= 3)
        def _():
            finish(i - 3)

        return carry

    lax.fori_loop(0, chunks + 2, flow, 0)

    finish(chunks - 1)
    value = mine[...]
    for i in range(1, n):
        l_copy(i).wait_recv()
        value = value + psq[i]
    value = jnp.sum(jnp.sum(value, axis=1, keepdims=True), axis=0, keepdims=True)
    loss[...] = jnp.broadcast_to(value * (0.5 * per_total), loss.shape)

    for u in range(1, side):
        p_first(u).wait_send()
    for v in range(1, side):
        for u in range(side):
            p_second(u, v).wait_send()
    for i in range(1, n):
        m_copy(i).wait_send()
        l_copy(i).wait_send()
    for i in range(1, n_mp):
        y_copy(i).wait_send()
    for c in range(zc):
        for i in range(n_mp - 1):
            for up in (True, False):
                @pl.when(z_sends(up, i))
                def _():
                    z_copy(up, i, c).wait_send()
        for i in range(n_mp):
            f_copy(i, c).wait_send()

            @pl.when(owner(i) != chip)
            def _():
                e_copy(i, zbuf.at[i, c], c).wait_send()

    @pl.when(is_low == 0)
    def _():
        t_copy().wait_send()

    w_swap.wait_send()
    n_copy.wait_send()
    n_copy.wait_recv()
    left_copy.wait()
    for i in range(1, nc):
        s_copy(i).wait_send()
        k_copy(i).wait_send()

    def drain(k, carry):
        for u in range(1, side):
            a_copy(k, u).wait_send()
            g_first(k, u).wait_send()
        for v in range(1, side):
            b_copy(k, v).wait_send()
            for u in range(side):
                g_second(k, u, v).wait_send()
        for u in range(side):
            for v in range(side):
                g_across(k, u, v).wait_send()
        o_copy(k).wait()
        return carry

    lax.fori_loop(0, chunks, drain, 0)


def run_block(patches, embed, weight, counts, targets, n, n_mp):
    length, rows = patches.shape
    piece = embed.shape[0]
    columns = weight.shape[2]
    heads = columns // HD
    nc = n // 2
    side = grid_side(nc)
    keep = rows * 3 // 4
    group = nc * keep
    block = n_mp * piece
    imgs = counts.shape[0]
    assert n % (2 * n_mp) == 0 and block == weight.shape[1]
    zc = 4 if piece % 64 == 0 else 1
    hp = 2 if heads % 2 == 0 else 1
    chunks = heads // hp
    wide = 3 * hp * HD
    dma = lambda *k: pltpu.SemaphoreType.DMA(k) if k else pltpu.SemaphoreType.DMA
    anywhere = pl.BlockSpec(memory_space=pl.ANY)
    vmem = pl.BlockSpec(memory_space=pltpu.VMEM)
    v = pltpu.VMEM
    return pl.pallas_call(
        functools.partial(block_kernel, n, n_mp, zc, hp),
        out_shape=(
            jax.ShapeDtypeStruct((2, block, group), BF16),
            jax.ShapeDtypeStruct((chunks, 2, nc, keep, wide), BF16),
            jax.ShapeDtypeStruct((8, 128), F32),
        ),
        in_specs=[anywhere, anywhere, anywhere, pl.BlockSpec(memory_space=pltpu.SMEM), anywhere],
        out_specs=(anywhere, anywhere, vmem),
        scratch_shapes=[
            v((nc, length, rows), BF16),
            v((n_mp, zc, piece // zc, length), BF16),
            v((2 * n_mp, zc, piece // zc, length), BF16),
            v((2,) + weight.shape, BF16),
            v((length, group), BF16),
            v((group, length), BF16),
            v((2, block, group), BF16),
            v((2, group + 16, block), BF16),
            v((group, 128), F32),
            v((group, 128), F32),
            v((nc, chunks, 8, HD), F32),
            v((nc, 8, group), F32),
            v((n, imgs, 128), jnp.int32),
            v((rows, columns), BF16),
            v((keep, columns), BF16),
            v((keep, columns), F32),
            v((keep, keep), F32),
            v((keep, HD), F32),
            v((chunks, nc, keep, wide), F32),
            v((chunks, side, side, keep, wide), BF16),
            v((chunks, side, side, keep, wide), BF16),
            v((chunks, side, keep, wide), BF16),
            v((chunks, keep, wide), F32),
            v((chunks, side, keep, wide), BF16),
            v((chunks, nc, keep, wide), BF16),
            v((8, 128), F32),
            v((n_mp, 8, 128), F32),
            v((n, 8, 128), F32),
            v((8, 128), F32),
            dma(), dma(), dma(),
            dma(n), dma(n),
            dma(side, side), dma(side, side),
            dma(n_mp, zc), dma(n_mp, zc), dma(n_mp, zc), dma(n_mp, zc),
            dma(n_mp, zc), dma(n_mp, zc), dma(zc),
            dma(n_mp, zc), dma(n_mp, zc),
            dma(), dma(), dma(),
            dma(nc), dma(nc), dma(nc), dma(nc),
            dma(), dma(),
            dma(chunks, side), dma(chunks, side),
            dma(chunks, side), dma(chunks, side),
            dma(chunks, side), dma(chunks, side),
            dma(chunks, side, side), dma(chunks, side, side),
            dma(chunks, side, side), dma(chunks, side, side),
            dma(n_mp), dma(n_mp), dma(n), dma(n),
            dma(chunks), dma(),
        ],
        compiler_params=pltpu.CompilerParams(
            collective_id=0, has_side_effects=True, vmem_limit_bytes=VMEM_BYTES
        ),
    )(patches, embed, weight, counts, targets)


def weight_grad_kernel(left, right, loss_in, out, loss_out, stage, sem):
    chunks, _, _, wide = stage.shape
    both = jnp.concatenate([left[0], left[1]], axis=1)
    copies = []
    for k in range(chunks):
        value = fdot(both, right[k])
        for s in range(3):
            stage[k, s] = value[:, s * wide:(s + 1) * wide]
        copies.append(pltpu.make_async_copy(stage.at[k], out.at[:, :, pl.ds(k * wide, wide)], sem.at[k]))
        copies[-1].start()
    loss_out[0, 0] = loss_in[0, 0]
    for copy in copies:
        copy.wait()


def weight_grad_of(left, grads, loss):
    _, block, group = left.shape
    chunks, wide = grads.shape[0], grads.shape[-1] // 3
    right = grads.reshape(chunks, 2 * group, 3 * wide)
    vmem = pl.BlockSpec(memory_space=pltpu.VMEM)
    smem = pl.BlockSpec(memory_space=pltpu.SMEM)
    return pl.pallas_call(
        weight_grad_kernel,
        out_shape=(
            jax.ShapeDtypeStruct((3, block, chunks * wide), F32),
            jax.ShapeDtypeStruct((1, 1), F32),
        ),
        in_specs=[vmem, vmem, smem],
        out_specs=(pl.BlockSpec(memory_space=pl.ANY), smem),
        scratch_shapes=[
            pltpu.VMEM((chunks, 3, block, wide), F32),
            pltpu.SemaphoreType.DMA((chunks,)),
        ],
        compiler_params=pltpu.CompilerParams(vmem_limit_bytes=VMEM_BYTES),
    )(left, right, loss)


def local(n, n_mp, patches, embed_weight, project_weight, patch_counts, segment_ids, targets):
    del segment_ids
    left, grads, loss = run_block(
        patches.T, embed_weight, jnp.transpose(project_weight, (1, 0, 2)), patch_counts, targets, n, n_mp
    )
    weight_grad, loss = weight_grad_of(left, grads, loss)
    return (jnp.transpose(weight_grad, (1, 0, 2)), loss.reshape(()))


def solution(mesh):
    in_specs = (
        P("dp", None),
        P(("mp", "dp"), None),
        P("dp", None, "mp"),
        P("dp"),
        P("dp"),
        P("dp", "mp"),
    )
    out_specs = (P("dp", None, "mp"), P())
    return jax.shard_map(
        functools.partial(local, mesh.shape["dp"], mesh.shape["mp"]), mesh=mesh, in_specs=in_specs, out_specs=out_specs, check_vma=False)
```
